256 devices in a mesh: tm: 32 (over x, z_hi, core), space: 8 (over y, z_lo).
Axes of the slice: x: 4, y: 4, z: 8 (z_hi: 4, z_lo: 2; z = z_hi * 2 + z_lo), core: 2. Of those that a mesh axis runs over, the one named last changes fastest.
Arguments:
- primal: float32 [256, 5, 64, 16, 128], P('tm', None, 'space'), may hold values from -2 to 2
- source: float32 [256, 5, 64, 16, 128], P('tm', None, 'space'), may hold values from -4 to 4
- guess: float32 [32, 5, 64, 16, 128], P('tm', None, 'space'), may hold values from -6 to 6
- mixing: float32 [5, 5], replicated, may hold values from -1 to 1.2
Outputs:
- fine_states: float32 [256, 5, 64, 16, 128], P('tm', None, 'space')
- coarse_residual: float32 [32, 5, 64, 16, 128], P('tm', None, 'space')
The draws below stay inside these ranges and needn't reach their ends.
All inputs are finite; a program needn't handle non-finite values.
Results may differ from the reference program's by a relative error of at most 0.00026.
Values sent between devices are 32-bit elements; how exact they have to be, the bound alone decides.
No kernel may reach another device: no remote copies, remote signals or barrier semaphores. Data moves between devices by JAX's collectives and lax.ppermute only.
A program may use at most 64 MiB of HBM per device.

```python
import jax
import jax.numpy as jnp
from jax import lax

FIELDS = 5
STEPS = 8
NY = 16
NZ = 128
NX = 64
BLOCKS = 32
NT = 256
N_TM = 32


def draw_mixing(key, part):
    keys = jax.random.split(jax.random.fold_in(key, 7), 4)
    order = jax.random.permutation(keys[0], FIELDS)
    slow_count = (FIELDS + 1) // 2
    slow_mask = (order < slow_count).astype(jnp.float32)
    slow_diag = jax.random.uniform(keys[1], (FIELDS,), jnp.float32, 1.02, 1.12)
    fast_diag = jax.random.uniform(keys[2], (FIELDS,), jnp.float32, 0.1, 0.35)
    diagonal = slow_mask * slow_diag + (1.0 - slow_mask) * fast_diag
    raw = 0.1 * jax.random.truncated_normal(keys[3], -3.0, 3.0, (FIELDS, FIELDS), jnp.float32)
    turning = raw - raw.T
    return jnp.diag(diagonal) + turning


def shard_levels(stream_key, dims, cuts, smallest, high):
    loudness, own = 1.0, jax.random.fold_in(stream_key, 6)
    for dim, shards_of in cuts:
        heights = jnp.exp(jax.random.uniform(jax.random.fold_in(own, dim), (shards_of,), jnp.float32, smallest / len(cuts), high / len(cuts)))
        loudness = loudness * jnp.repeat(heights, dims[dim] // shards_of).reshape([-1 if axis == dim else 1 for axis in range(len(dims))])
    return loudness


def normal_values(own_key, extent, scale, bound, pieces=(), kind=jnp.bfloat16):
    values = jax.random.normal(own_key, extent, jnp.float32) * scale
    if len(pieces) > 0:
        values = shard_levels(own_key, extent, pieces, -0.22, 0.18) * values
    return jnp.clip(values, min=-bound, max=bound).astype(kind)


def setup_inputs(seed: int = 0) -> dict:
    splits = jax.random.split(jax.random.key(seed), 5)
    primal = normal_values(splits[0], (NT, FIELDS, NX, NY, NZ), 0.35, 2.0, ((0, 32), (2, 8)), jnp.float32)
    source = normal_values(splits[1], (NT, FIELDS, NX, NY, NZ), 0.5, 4.0, ((0, 32), (2, 8)), jnp.float32)
    guess = normal_values(splits[2], (BLOCKS, FIELDS, NX, NY, NZ), 1.0, 6.0, ((0, 32), (2, 8)), jnp.float32)
    mixing = draw_mixing(jax.random.fold_in(splits[4], 71), 0)
    return dict(primal=primal, source=source, guess=guess, mixing=mixing)


DIFFUSION = 0.1
RATE = 0.25
COARSE_STEP = 0.75


def apply_mix(mixing, field):
    return jnp.einsum("ij,...jxyz->...ixyz", mixing, field, precision=lax.Precision.HIGHEST)


def slopes(mixing, state):
    tilted = jnp.tanh(apply_mix(mixing, state))
    return 1.0 - tilted * tilted


def laplace(field, across):
    widths = [(0, 0)] * (field.ndim - 2) + [(1, 1), (0, 0)]
    padded = jnp.pad(field, widths)
    total = across + padded[..., 2:, :] + padded[..., :-2, :]
    total = total + jnp.roll(field, 1, -1) + jnp.roll(field, -1, -1)
    return total - 6.0 * field


def advance(mixing, state, field, across):
    return field + DIFFUSION * laplace(field, across) + RATE * (slopes(mixing, state) * apply_mix(mixing, field) - field)


def march(mixing, states, sources, start, count):
    field = start
    marched = []
    for column in range(count):
        across = jnp.roll(field, 1, -3) + jnp.roll(field, -1, -3)
        field = advance(mixing, states[:, column], field, across)
        if column + 1 < STEPS:
            field = field + sources[:, column + 1]
        marched.append(field)
    return marched


def reference(primal, source, guess, mixing):
    shape = (N_TM, STEPS) + primal.shape[1:]
    states = primal.reshape(shape)
    sources = source.reshape(shape)
    ended = march(mixing, states, sources, guess, STEPS)[-1]
    relaxed = jnp.concatenate([guess[:1], ended[:-1] + sources[1:, 0]], axis=0)
    ended_again = march(mixing, states, sources, relaxed, STEPS)[-1]
    residual = jnp.concatenate([sources[:1, 0], ended_again[:-1] + sources[1:, 0] - relaxed[1:]], axis=0)
    coarse_slope = slopes(mixing, states[:, 0])

    def coarse_turn(error, inputs):
        slope_here, resid_next = inputs
        moved = error + COARSE_STEP * (slope_here * apply_mix(mixing, error) - error)
        following = moved + resid_next
        return following, following

    start_error = residual[0]
    last_error, errors = lax.scan(coarse_turn, start_error, (coarse_slope[:-1], residual[1:]))
    errors = jnp.concatenate([start_error[None], errors], axis=0)
    corrected = relaxed + errors
    finals = march(mixing, states, sources, corrected, STEPS - 1)
    fine_states = jnp.stack([corrected] + finals, axis=1).reshape(primal.shape)
    return fine_states, residual
```

```python
import functools

import jax
import jax.numpy as jnp
from jax import lax
from jax.experimental import pallas as pl
from jax.experimental.pallas import tpu as pltpu
from jax.sharding import PartitionSpec as P

STEPS = 8
FIELDS = 5
WIDE = 8
DIFFUSION = 0.1
RATE = 0.25
COARSE_STEP = 0.75
KEEP = 1.0 - 6.0 * DIFFUSION - RATE
REACH = [min(m, STEPS - 1 - m) for m in range(STEPS)]
REACH_AT = [sum(REACH[:m]) for m in range(STEPS)]
PACKED = sum(REACH)
HALO = max(min(m + 1, STEPS - 1 - m) for m in range(STEPS))


def mixed(mix, fields):
    out = []
    for i in range(FIELDS):
        total = mix[i][0] * fields[0]
        for j in range(1, FIELDS):
            total = total + mix[i][j] * fields[j]
        out.append(total)
    return out


def scalars(mix_ref):
    return [[mix_ref[i, j] for j in range(FIELDS)] for i in range(FIELDS)]


def stepped(mix, field, beside, slope, source):
    row = lax.broadcasted_iota(jnp.int32, (16, 128), 0)
    first, last = row == 0, row == 15
    out = []
    for f, turned in enumerate(mixed(mix, field)):
        v = field[f]
        around = pltpu.roll(v, 1, 1) + pltpu.roll(v, 127, 1)
        around = around + jnp.where(first, 0.0, pltpu.roll(v, 1, 0))
        around = around + jnp.where(last, 0.0, pltpu.roll(v, 15, 0))
        if beside is not None:
            around = around + beside[f]
        new = KEEP * v + DIFFUSION * around + slope[f] * turned
        out.append(new if source is None else new + source[f])
    return out


def prepare_kernel(mix_ref, primal_ref, slope_ref, up_ref, down_ref):
    mix = scalars(mix_ref)

    def plane(n, carry):
        t, x = n // WIDE, n % WIDE
        for f, value in enumerate(mixed(mix, [primal_ref[t, f, x] for f in range(FIELDS)])):
            tilted = jnp.tanh(value)
            slope_ref[t, f, x] = RATE - RATE * (tilted * tilted)
        return carry

    lax.fori_loop(0, STEPS * WIDE, plane, 0)
    for f in range(FIELDS):
        for m in range(STEPS):
            n, a = REACH[m], REACH_AT[m]
            if n > 0:
                up_ref[f, a : a + n] = slope_ref[m, f, WIDE - n :]
                down_ref[f, a : a + n] = slope_ref[m, f, :n]


def alone_kernel(count, mix_ref, start_ref, slope_ref, source_ref, up_ref, down_ref, one, two):
    mix = scalars(mix_ref)
    for f in range(FIELDS):
        down_ref[f, 0] = start_ref[f, 0]
        up_ref[f, 0] = start_ref[f, WIDE - 1]
    buffers = (one, two)
    for m in range(count - 1):
        here = start_ref if m == 0 else buffers[m % 2]
        there = buffers[(m + 1) % 2]
        for x in range(WIDE):
            if not (x >= m + 1 or x <= WIDE - 2 - m):
                continue
            field = [here[f, x] for f in range(FIELDS)]
            if x == 0:
                beside = [here[f, 1] for f in range(FIELDS)]
            elif x == WIDE - 1:
                beside = [here[f, WIDE - 2] for f in range(FIELDS)]
            else:
                beside = [here[f, x - 1] + here[f, x + 1] for f in range(FIELDS)]
            new = stepped(
                mix,
                field,
                beside,
                [slope_ref[m, f, x] for f in range(FIELDS)],
                [source_ref[m + 1, f, x] for f in range(FIELDS)],
            )
            for f in range(FIELDS):
                there[f, x] = new[f]
                if x == 0:
                    down_ref[f, m + 1] = new[f]
                if x == WIDE - 1:
                    up_ref[f, m + 1] = new[f]


def march_kernel(count, keep_all, mix_ref, start_ref, low_ref, high_ref, slope_ref, source_ref, packed_low, packed_high, out_ref, one, two, added_one, added_two):
    mix = scalars(mix_ref)
    fields = range(FIELDS)
    if keep_all:
        for f in fields:
            out_ref[0, f] = start_ref[f]
    buffers, extras = (one, two), (added_one, added_two)
    sides = (
        (0, low_ref, packed_low, lambda n, p: n - p),
        (WIDE - 1, high_ref, packed_high, lambda n, p: p - 1),
    )
    for m in range(count):
        here = start_ref if m == 0 else buffers[m % 2]
        there, here_added, there_added = buffers[(m + 1) % 2], extras[m % 2], extras[(m + 1) % 2]
        last = m + 1 == count

        def own(x, beside):
            field = [here[f, x] for f in fields]
            slope = [slope_ref[m, f, x] for f in fields]
            source = [source_ref[m + 1, f, x] for f in fields] if m + 1 < STEPS else None
            new = stepped(mix, field, beside, slope, source)
            for f in fields:
                if not last:
                    there[f, x] = new[f]
                if keep_all:
                    out_ref[m + 1, f, x] = new[f]
                elif last:
                    out_ref[f, x] = new[f]

        for side, (edge, alone, packed, place) in enumerate(sides):
            inner = edge + 1 if edge == 0 else edge - 1
            beyond = [alone[f, m] for f in fields]
            if m > 0:
                beyond = [beyond[f] + here_added[side, f, 0] for f in fields]
            own(edge, [here[f, inner] + beyond[f] for f in fields])
            for p in range(1, min(m + 1, count - 1 - m) + 1):
                nearer = [here[f, edge] if p == 1 else here_added[side, f, p - 2] for f in fields]
                if p == m + 1:
                    for f in fields:
                        there_added[side, f, p - 1] = DIFFUSION * nearer[f]
                    continue
                beside = nearer
                if p + 1 <= m:
                    beside = [nearer[f] + here_added[side, f, p] for f in fields]
                at = REACH_AT[m] + place(REACH[m], p)
                new = stepped(
                    mix,
                    [here_added[side, f, p - 1] for f in fields],
                    beside,
                    [packed[f, at] for f in fields],
                    None,
                )
                for f in fields:
                    there_added[side, f, p - 1] = new[f]

        def inside(i, carry):
            for k in range(3):
                x = 1 + 3 * i + k
                own(x, [here[f, x - 1] + here[f, x + 1] for f in fields])
            return carry

        lax.fori_loop(0, 2, inside, 0)


def scan_kernel(mix_ref, slope_ref, resid_ref, error_ref):
    blocks = resid_ref.shape[0]
    mix = scalars(mix_ref)
    error = [resid_ref[0, f] for f in range(FIELDS)]
    for f in range(FIELDS):
        error_ref[0, f] = error[f]

    def turn(i, error):
        new = []
        for f, turned in enumerate(mixed(mix, error)):
            scaled = (COARSE_STEP / RATE) * slope_ref[i, f]
            new.append((1.0 - COARSE_STEP) * error[f] + scaled * turned + resid_ref[i + 1, f])
            error_ref[i + 1, f] = new[f]
        return tuple(new)

    lax.fori_loop(0, blocks - 1, turn, tuple(error))


VMEM = functools.partial(pl.BlockSpec, memory_space=pltpu.VMEM)
SMEM = functools.partial(pl.BlockSpec, memory_space=pltpu.SMEM)


def call(kernel, out, operands, planes, scratch=(), name=None):
    read = sum(4 * operand.size for operand in operands)
    written = sum(4 * leaf.size for leaf in jax.tree.leaves(out))
    return pl.pallas_call(
        kernel,
        out_shape=out,
        in_specs=[SMEM()] + [VMEM()] * (len(operands) - 1),
        out_specs=jax.tree.map(lambda _: VMEM(), out),
        scratch_shapes=list(scratch),
        compiler_params=pltpu.CompilerParams(vmem_limit_bytes=20 << 20),
        cost_estimate=pl.CostEstimate(
            flops=planes * FIELDS * 2048 * 25, bytes_accessed=read + written, transcendentals=0
        ),
        name=name,
    )(*operands)


def struct(*shape):
    return jax.ShapeDtypeStruct(shape, jnp.float32)


def from_behind(array):
    count = lax.axis_size("tm")
    return lax.ppermute(array, "tm", [(i, i + 1) for i in range(count - 1)])


def exchange(up, down):
    count = lax.axis_size("space")
    forward = [(i, (i + 1) % count) for i in range(count)]
    backward = [(b, a) for a, b in forward]
    return lax.ppermute(up, "space", forward), lax.ppermute(down, "space", backward)


def chunked(slab, parts):
    return slab.reshape(FIELDS, parts, -1, 128).transpose(1, 0, 2, 3)


def per_device(primal, source, guess, mixing):
    parts = lax.axis_size("tm")
    leading = lax.axis_index("tm") == 0
    cells = primal.shape[2:]
    slab = (FIELDS,) + cells
    plane = cells[1:]
    packed = struct(FIELDS, PACKED, *plane)
    slope, up, down = call(
        prepare_kernel,
        (struct(*primal.shape), packed, packed),
        (mixing, primal),
        STEPS * WIDE,
        name="prepare",
    )
    packed_low, packed_high = exchange(up, down)
    slope_share = lax.all_to_all(chunked(slope[0], parts), "tm", 0, 0)

    def march(start, count, keep_all, name):
        ends = struct(FIELDS, count, *plane)
        room = pltpu.VMEM(slab, jnp.float32)
        up, down = call(
            functools.partial(alone_kernel, count),
            (ends, ends),
            (mixing, start, slope, source),
            44,
            scratch=[room, room],
            name="alone_" + name,
        )
        low, high = exchange(up, down)
        extra = pltpu.VMEM((2, FIELDS, HALO) + plane, jnp.float32)
        return call(
            functools.partial(march_kernel, count, keep_all),
            struct(STEPS, *slab) if keep_all else struct(*slab),
            (mixing, start, low, high, slope, source, packed_low, packed_high),
            88,
            scratch=[room, room, extra, extra],
            name="march_" + name,
        )

    start = guess[0]
    ended = march(start, STEPS, False, "guess")
    relaxed = jnp.where(leading, start, from_behind(ended) + source[0])
    ended_again = march(relaxed, STEPS, False, "relaxed")
    residual = jnp.where(leading, source[0], from_behind(ended_again) + source[0] - relaxed)
    resid_share = lax.all_to_all(chunked(residual, parts), "tm", 0, 0)
    error_share = call(
        scan_kernel, struct(*resid_share.shape), (mixing, slope_share, resid_share), 16, name="scan"
    )
    error = lax.all_to_all(error_share, "tm", 0, 0)
    error = error.transpose(1, 0, 2, 3).reshape(slab)
    corrected = relaxed + error
    fine_states = march(corrected, STEPS - 1, True, "corrected")
    return fine_states, residual[None]


def solution(mesh):
    split = P("tm", None, "space", None, None)
    return jax.shard_map(
        per_device,
        mesh=mesh,
        in_specs=(split, split, split, P()),
        out_specs=(split, split),
        check_vma=False,
    )
```

```python
import functools

import jax
import jax.numpy as jnp
from jax import lax
from jax.experimental import pallas as pl
from jax.experimental.pallas import tpu as pltpu
from jax.sharding import PartitionSpec as P


STEPS = 8
FIELDS = 5
WIDE = 8
DIFFUSION = 0.1
RATE = 0.25
COARSE_STEP = 0.75
KEEP = 1.0 - 6.0 * DIFFUSION - RATE
REACH = [min(m, STEPS - 1 - m) for m in range(STEPS)]
REACH_AT = [sum(REACH[:m]) for m in range(STEPS)]
PACKED = sum(REACH)
HALF = STEPS // 2
HALO = max(min(m + 1, STEPS - 1 - m) for m in range(STEPS))


def mixed(mix, fields):
    out = []
    for i in range(FIELDS):
        total = mix[i][0] * fields[0]
        for j in range(1, FIELDS):
            total = total + mix[i][j] * fields[j]
        out.append(total)
    return out


def scalars(mix_ref):
    return [[mix_ref[i, j] for j in range(FIELDS)] for i in range(FIELDS)]


def wall_neighbours(v):
    row = lax.broadcasted_iota(jnp.int32, (8, 128), 0)
    first, last = row == 0, row == 7
    a, b = v[:8], v[8:]
    a_next, b_next = pltpu.roll(a, 1, 0), pltpu.roll(b, 1, 0)
    a_prev, b_prev = pltpu.roll(a, 7, 0), pltpu.roll(b, 7, 0)
    upper = jnp.where(first, 0.0, a_next) + jnp.where(last, b_prev, a_prev)
    lower = jnp.where(first, a_next, b_next) + jnp.where(last, 0.0, b_prev)
    return jnp.concatenate([upper, lower], axis=0)


def stepped(mix, field, beside, slope, source):
    out = []
    for f, turned in enumerate(mixed(mix, field)):
        v = field[f]
        around = pltpu.roll(v, 1, 1) + pltpu.roll(v, 127, 1) + wall_neighbours(v)
        around = around + beside[f]
        new = KEEP * v + DIFFUSION * around + slope[f] * turned
        out.append(new if source is None else new + source[f])
    return out


class Streamed:
    def __init__(self, hbm, room, sems, wanted):
        self.copies = {t: pltpu.make_async_copy(hbm.at[t], room.at[t], sems.at[t]) for t in wanted}
        for copy in self.copies.values():
            copy.start()

    def ready(self, t):
        if t in self.copies:
            self.copies.pop(t).wait()


def slopes(mix, state):
    out = []
    for value in mixed(mix, state):
        tilted = jnp.tanh(value)
        out.append(RATE - RATE * (tilted * tilted))
    return out


def border_kernel(mix_ref, primal_hbm, up_ref, down_ref, up_state, down_state, sems):
    mix = scalars(mix_ref)
    copies = []
    for m in range(STEPS):
        n, a = REACH[m], REACH_AT[m]
        if n > 0:
            ends = (pl.ds(WIDE - n, n), up_state), (pl.ds(0, n), down_state)
            for planes, state in ends:
                copies.append(
                    pltpu.make_async_copy(
                        primal_hbm.at[m, :, planes], state.at[:, a : a + n], sems.at[len(copies)]
                    )
                )
    for copy in copies:
        copy.start()
    for copy in copies:
        copy.wait()
    for state, out_ref in ((up_state, up_ref), (down_state, down_ref)):

        def plane(n, carry):
            for k in range(2):
                x = 2 * n + k
                for f, value in enumerate(slopes(mix, [state[f, x] for f in range(FIELDS)])):
                    out_ref[f, x] = value
            return carry

        lax.fori_loop(0, PACKED // 2, plane, 0)


def shares(part):
    return [(part * x + q, x, 4 * q) for x in range(WIDE) for q in range(part)]


def alone_step(mix, m, here, there, slope_ref, source_ref, ends):
    for x in range(WIDE):
        if not (x >= m + 1 or x <= WIDE - 2 - m):
            continue
        field = [here[f, x] for f in range(FIELDS)]
        if x == 0:
            beside = [here[f, 1] for f in range(FIELDS)]
        elif x == WIDE - 1:
            beside = [here[f, WIDE - 2] for f in range(FIELDS)]
        else:
            beside = [here[f, x - 1] + here[f, x + 1] for f in range(FIELDS)]
        slope = [slope_ref[m, f, x] for f in range(FIELDS)]
        source = None
        if source_ref is not None:
            source = [source_ref[m + 1, f, x] for f in range(FIELDS)]
        new = stepped(mix, field, beside, slope, source)
        for f in range(FIELDS):
            there[f, x] = new[f]
            if x == 0 or x == WIDE - 1:
                ends[(m + 1) // HALF][int(x == 0)][f, (m + 1) % HALF] = new[f]


def guess_kernel(mix_ref, primal_hbm, source_hbm, guess_ref, slope_ref, share_ref, up_one, down_one, up_two, down_two, primal, source_ref, one, two, sems):
    mix = scalars(mix_ref)
    primal_in = Streamed(primal_hbm, primal, sems.at[0], range(STEPS))
    source_in = Streamed(source_hbm, source_ref, sems.at[1], range(1, STEPS))
    start_ref = guess_ref.at[0]
    ends = [(up_one, down_one), (up_two, down_two)]
    for f in range(FIELDS):
        down_one[f, 0] = start_ref[f, 0]
        up_one[f, 0] = start_ref[f, WIDE - 1]
    buffers = (one, two)
    for t in range(STEPS):
        primal_in.ready(t)

        def plane(n, carry):
            for k in range(2):
                x = 2 * n + k
                state = [primal[t, f, x] for f in range(FIELDS)]
                for f, value in enumerate(slopes(mix, state)):
                    slope_ref[t, f, x] = value
            return carry

        lax.fori_loop(0, WIDE // 2, plane, 0)
        if t == 0:
            for share, x, row in shares(4):
                for f in range(FIELDS):
                    share_ref[share, f] = slope_ref[0, f, x, row : row + 4]
        source_in.ready(t + 1)
        if t + 1 < STEPS:
            here = start_ref if t == 0 else buffers[t % 2]
            alone_step(mix, t, here, buffers[(t + 1) % 2], slope_ref, source_ref, ends)


def relaxed_kernel(mix_ref, leads_ref, source_hbm, ended_ref, guess_ref, slope_ref, relaxed_hbm, change_ref, middle_ref, up_ref, down_ref, source_ref, relaxed_ref, one, two, sems):
    source_in = Streamed(source_hbm, source_ref, sems, [0])
    mix = scalars(mix_ref)
    leads = leads_ref[0] == 1
    source_in.ready(0)
    for f in range(FIELDS):
        for x in range(WIDE):
            before = guess_ref[0, f, x]
            after = jnp.where(leads, before, ended_ref[f, x] + source_ref[0, f, x])
            relaxed_ref[f, x] = after
            change_ref[f, x] = after - before
        down_ref[f, 0] = change_ref[f, 0]
        up_ref[f, 0] = change_ref[f, WIDE - 1]
    relaxed_out = pltpu.make_async_copy(relaxed_ref, relaxed_hbm, sems.at[1])
    relaxed_out.start()
    buffers = (one, two)
    for m in range(HALF - 1):
        here = change_ref if m == 0 else buffers[m % 2]
        there = middle_ref if m == HALF - 2 else buffers[(m + 1) % 2]
        alone_step(mix, m, here, there, slope_ref, None, [(up_ref, down_ref)])
    relaxed_out.wait()


def rest_kernel(count, forced, mix_ref, source_hbm, middle_ref, slope_ref, up_ref, down_ref, one, two, source_ref, sems):
    source_in = Streamed(source_hbm, source_ref, sems, range(HALF, count) if forced else [])
    mix = scalars(mix_ref)
    buffers = (one, two)
    for m in range(HALF - 1, count - 1):
        source_in.ready(m + 1)
        here = middle_ref if m == HALF - 1 else buffers[m % 2]
        source = source_ref if forced else None
        alone_step(mix, m, here, buffers[(m + 1) % 2], slope_ref, source, [None, (up_ref, down_ref)])


def corrected_kernel(mix_ref, leads_ref, relaxed_hbm, source_hbm, share_ref, slope_ref, corrected_ref, middle_ref, up_ref, down_ref, relaxed_ref, source_ref, one, two, sems):
    relaxed_in = pltpu.make_async_copy(relaxed_hbm, relaxed_ref, sems.at[STEPS])
    relaxed_in.start()
    source_in = Streamed(source_hbm, source_ref, sems, range(HALF))
    mix = scalars(mix_ref)
    leads = leads_ref[0] == 1
    relaxed_in.wait()
    source_in.ready(0)
    for share, x, row in shares(4):
        for f in range(FIELDS):
            rows = slice(row, row + 4)
            error = jnp.where(leads, source_ref[0, f, x, rows], share_ref[share, f])
            corrected_ref[f, x, rows] = relaxed_ref[f, x, rows] + error
    for f in range(FIELDS):
        down_ref[f, 0] = corrected_ref[f, 0]
        up_ref[f, 0] = corrected_ref[f, WIDE - 1]
    buffers = (one, two)
    for m in range(HALF - 1):
        source_in.ready(m + 1)
        here = corrected_ref if m == 0 else buffers[m % 2]
        there = middle_ref if m == HALF - 2 else buffers[(m + 1) % 2]
        alone_step(mix, m, here, there, slope_ref, source_ref, [(up_ref, down_ref)])


def march_steps(count, steps, forced, done, step_opens, step_ends, mix, start_ref, start_added, low_ref, high_ref, slope_ref, source_ref, packed_low, packed_high, one, two, added_one, added_two, middle=None):
    fields = range(FIELDS)
    buffers, extras = (one, two), (added_one, added_two)
    sides = (
        (0, low_ref, packed_low, lambda n, p: n - p),
        (WIDE - 1, high_ref, packed_high, lambda n, p: p - 1),
    )
    for m in steps:
        here = start_ref if m == steps[0] else buffers[m % 2]
        step_opens(m)
        here_added = start_added if m == steps[0] else extras[m % 2]
        there, there_added = buffers[(m + 1) % 2], extras[(m + 1) % 2]
        if middle is not None and m == steps[-1]:
            there, there_added = middle
        last = m + 1 == count

        def own(x, beside):
            field = [here[f, x] for f in fields]
            slope = [slope_ref[m, f, x] for f in fields]
            source = [source_ref[m + 1, f, x] for f in fields] if forced and m + 1 < STEPS else None
            new = stepped(mix, field, beside, slope, source)
            for f in fields:
                if not last:
                    there[f, x] = new[f]
                done(m + 1, f, x, new[f])

        for side, (edge, alone, packed, place) in enumerate(sides):
            inner = edge + 1 if edge == 0 else edge - 1
            beyond = [alone[m // HALF][f, m % HALF] for f in fields]
            if m > 0:
                beyond = [beyond[f] + here_added[side, f, 0] for f in fields]
            own(edge, [here[f, inner] + beyond[f] for f in fields])
            for p in range(1, min(m + 1, count - 1 - m) + 1):
                nearer = [here[f, edge] if p == 1 else here_added[side, f, p - 2] for f in fields]
                if p == m + 1:
                    for f in fields:
                        there_added[side, f, p - 1] = DIFFUSION * nearer[f]
                    continue
                beside = nearer
                if p + 1 <= m:
                    beside = [nearer[f] + here_added[side, f, p] for f in fields]
                at = REACH_AT[m] + place(REACH[m], p)
                new = stepped(
                    mix,
                    [here_added[side, f, p - 1] for f in fields],
                    beside,
                    [packed[f, at] for f in fields],
                    None,
                )
                for f in fields:
                    there_added[side, f, p - 1] = new[f]

        def inside(i, carry):
            for k in range(3):
                x = 1 + 3 * i + k
                own(x, [here[f, x - 1] + here[f, x + 1] for f in fields])
            return carry

        lax.fori_loop(0, 2, inside, 0)
        step_ends(m)


def nothing(m):
    pass


def march_first_kernel(count, forced, mix_ref, source_hbm, start_ref, low_ref, high_ref, slope_ref, packed_low, packed_high, middle_ref, middle_added, *rest):
    later_ref, (one, two, added_one, added_two, source_ref, sems) = rest[0], rest[-6:]
    source_in = Streamed(source_hbm, source_ref, sems, range(1, HALF + 1) if forced else [])
    later = pltpu.make_async_copy(source_hbm.at[HALF + 1 :], later_ref, sems.at[HALF + 1]) if forced else None
    if forced:
        later.start()
    march_steps(
        count, range(HALF), forced, lambda *_: None, lambda m: source_in.ready(m + 1), nothing, scalars(mix_ref),
        start_ref, None, (low_ref, None), (high_ref, None), slope_ref, source_ref, packed_low, packed_high,
        one, two, added_one, added_two, (middle_ref, middle_added),
    )
    if forced:
        later.wait()


class Later:
    def __init__(self, ref):
        self.ref = ref

    def __getitem__(self, index):
        return self.ref[(index[0] - HALF - 1,) + index[1:]]


def end_kernel(mix_ref, later_ref, middle_ref, middle_added, low_ref, high_ref, slope_ref, packed_low, packed_high, out_ref, one, two, added_one, added_two):
    def done(step, f, x, value):
        if step == STEPS:
            out_ref[f, x] = value

    march_steps(
        STEPS, range(HALF, STEPS), True, done, nothing, nothing, scalars(mix_ref),
        middle_ref, middle_added, (None, low_ref), (None, high_ref), slope_ref, Later(later_ref), packed_low, packed_high,
        one, two, added_one, added_two,
    )


def change_kernel(mix_ref, leads_ref, source_hbm, middle_ref, middle_added, low_ref, high_ref, slope_ref, packed_low, packed_high, out_hbm, share_ref, one, two, added_one, added_two, source_ref, out_ref, sems):
    source_in = Streamed(source_hbm, source_ref, sems, [0])
    mix = scalars(mix_ref)

    def done(step, f, x, value):
        if step == STEPS:
            out_ref[f, x] = value

    march_steps(
        STEPS, range(HALF, STEPS), False, done, nothing, nothing, mix,
        middle_ref, middle_added, (None, low_ref), (None, high_ref), slope_ref, None, packed_low, packed_high,
        one, two, added_one, added_two,
    )
    out = pltpu.make_async_copy(out_ref, out_hbm, sems.at[1])
    out.start()
    source_in.ready(0)
    leads = leads_ref[0] == 1
    for x in range(WIDE):
        error = [source_ref[0, f, x] for f in range(FIELDS)]
        slope = [slope_ref[0, f, x] for f in range(FIELDS)]
        moved = coarse_turn(mix, error, slope)
        for f in range(FIELDS):
            value = out_ref[f, x]
            value = jnp.where(leads, moved[f] + value, value)
            for q in range(4):
                share_ref[4 * x + q, f] = value[4 * q : 4 * q + 4]
    out.wait()


def states_first_kernel(mix_ref, source_hbm, start_ref, low_ref, high_ref, slope_ref, packed_low, packed_high, out_hbm, middle_ref, middle_added, later_ref, one, two, added_one, added_two, source_ref, out_ref, sems, out_sems):
    source_in = Streamed(source_hbm, source_ref, sems, range(1, HALF + 1))
    later = pltpu.make_async_copy(source_hbm.at[HALF + 1 :], later_ref, sems.at[HALF + 1])
    later.start()
    outs = [
        pltpu.make_async_copy(start_ref if t == 0 else out_ref.at[t], out_hbm.at[t], out_sems.at[t])
        for t in range(HALF + 1)
    ]
    outs[0].start()

    def done(step, f, x, value):
        out_ref[step, f, x] = value

    march_steps(
        STEPS - 1, range(HALF), True, done, lambda m: source_in.ready(m + 1), lambda m: outs[m + 1].start(),
        scalars(mix_ref),
        start_ref, None, (low_ref, None), (high_ref, None), slope_ref, source_ref, packed_low, packed_high,
        one, two, added_one, added_two, (middle_ref, middle_added),
    )
    later.wait()
    for out in outs:
        out.wait()


def states_rest_kernel(mix_ref, earlier_hbm, later_ref, middle_ref, middle_added, low_ref, high_ref, slope_ref, packed_low, packed_high, out_hbm, one, two, added_one, added_two, out_ref, out_sems):
    outs = {
        t: pltpu.make_async_copy(out_ref.at[t], out_hbm.at[t], out_sems.at[t])
        for t in range(HALF + 1, STEPS)
    }

    def done(step, f, x, value):
        out_ref[step, f, x] = value

    march_steps(
        STEPS - 1, range(HALF, STEPS - 1), True, done, nothing, lambda m: outs[m + 1].start(), scalars(mix_ref),
        middle_ref, middle_added, (None, low_ref), (None, high_ref), slope_ref, Later(later_ref),
        packed_low, packed_high, one, two, added_one, added_two,
    )
    for out in outs.values():
        out.wait()


def coarse_turn(mix, error, slope):
    out = []
    for f, turned in enumerate(mixed(mix, error)):
        out.append((1.0 - COARSE_STEP) * error[f] + (COARSE_STEP / RATE) * slope[f] * turned)
    return out


def scan_kernel(mix_ref, slope_ref, resid_ref, error_ref):
    mix = scalars(mix_ref)
    blocks = resid_ref.shape[0]
    error = tuple(resid_ref[0, f] for f in range(FIELDS))
    for f in range(FIELDS):
        error_ref[0, f] = error[f]
        error_ref[1, f] = error[f]

    def turn(i, error):
        moved = coarse_turn(mix, error, [slope_ref[i, f] for f in range(FIELDS)])
        new = tuple(moved[f] + resid_ref[i, f] for f in range(FIELDS))
        for f in range(FIELDS):
            error_ref[i + 1, f] = new[f]
        return new

    lax.fori_loop(1, blocks - 1, turn, error)


VMEM = pl.BlockSpec(memory_space=pltpu.VMEM)
SMEM = pl.BlockSpec(memory_space=pltpu.SMEM)
HBM = pl.BlockSpec(memory_space=pltpu.HBM)


def call(kernel, out, operands, places, planes, scratch=(), first_out=None, alias=None):
    read = sum(4 * operand.size for operand in operands)
    written = sum(4 * leaf.size for leaf in jax.tree.leaves(out))
    if first_out is not None:
        out = (pltpu.HBM(out[0].shape, out[0].dtype),) + tuple(out[1:])
    return pl.pallas_call(
        kernel,
        input_output_aliases=alias or {},
        out_shape=out,
        in_specs=places + [VMEM] * (len(operands) - len(places)),
        out_specs=[first_out or VMEM] + [VMEM] * (len(out) - 1),
        scratch_shapes=list(scratch),
        compiler_params=pltpu.CompilerParams(vmem_limit_bytes=20 << 20),
        cost_estimate=pl.CostEstimate(
            flops=planes * FIELDS * 2048 * 25, bytes_accessed=read + written, transcendentals=0
        ),
    )(*operands)


def in_hbm(array):
    return pltpu.with_memory_space_constraint(array, pltpu.HBM)


def struct(*shape):
    return jax.ShapeDtypeStruct(shape, jnp.float32)


def from_behind(array):
    count = lax.axis_size("tm")
    return lax.ppermute(array, "tm", [(i, i + 1) for i in range(count - 1)])


def exchange(up, down):
    count = lax.axis_size("space")
    forward = [(i, (i + 1) % count) for i in range(count)]
    backward = [(b, a) for a, b in forward]
    return lax.ppermute(up, "space", forward), lax.ppermute(down, "space", backward)


def per_device(primal, source, guess, mixing):
    parts = lax.axis_size("tm")
    leading = lax.axis_index("tm") == 0
    leads = leading.astype(jnp.int32)[None]
    plane = primal.shape[3:]
    slab = struct(*primal.shape[1:])
    whole = struct(*primal.shape)
    share = struct(parts, FIELDS, 4, plane[1])
    room = pltpu.VMEM(slab.shape, jnp.float32)
    extra = pltpu.VMEM((2, FIELDS, HALO) + plane, jnp.float32)
    march_room = [room, room, extra, extra]
    packed = struct(FIELDS, PACKED, *plane)

    packed_room = pltpu.VMEM(packed.shape, jnp.float32)
    up, down = call(
        border_kernel,
        (packed, packed),
        (mixing, in_hbm(primal)),
        [SMEM, HBM],
        2 * PACKED,
        scratch=[packed_room, packed_room, pltpu.SemaphoreType.DMA((2 * STEPS,))],
    )
    packed_low, packed_high = exchange(up, down)
    first_source = source[0]
    primal, source = in_hbm(primal), in_hbm(source)
    stream = [pltpu.VMEM(whole.shape, jnp.float32), pltpu.SemaphoreType.DMA((STEPS,))]
    half, rest = struct(FIELDS, HALF, *plane), struct(FIELDS, HALF - 1, *plane)
    added = struct(2, FIELDS, HALO, *plane)

    def march_first(start, low, high, forced):
        later = (struct(STEPS - HALF - 1, *slab.shape),) if forced else ()
        return call(
            functools.partial(march_first_kernel, STEPS, forced),
            (slab, added) + later,
            (mixing, source, start, low, high, slope, packed_low, packed_high),
            [SMEM, HBM],
            42,
            scratch=march_room + stream,
        )

    slope, slope_share, up, down, up_rest, down_rest = call(
        guess_kernel,
        (whole, share, half, half, half, half),
        (mixing, primal, source, guess),
        [SMEM, HBM, HBM],
        100,
        scratch=[stream[0], stream[0], room, room, pltpu.SemaphoreType.DMA((2, STEPS))],
    )
    low, high = exchange(up, down)
    low_rest, high_rest = exchange(up_rest, down_rest)
    middle, middle_added, later = march_first(guess[0], low, high, True)
    (ended,) = call(
        end_kernel,
        (slab,),
        (mixing, later, middle, middle_added, low_rest, high_rest, slope, packed_low, packed_high),
        [SMEM],
        46,
        scratch=march_room,
    )
    ended = from_behind(ended)
    slope_shares = lax.all_to_all(slope_share, "tm", 0, 0)
    relaxed, change, middle, up, down = call(
        relaxed_kernel,
        (slab, slab, slab, half, half),
        (mixing, leads, source, ended, guess, slope),
        [SMEM, SMEM, HBM],
        30,
        scratch=[pltpu.VMEM((1,) + slab.shape, jnp.float32), room, room, room, stream[1]],
        first_out=HBM,
    )
    low, high = exchange(up, down)
    up_rest, down_rest = call(
        functools.partial(rest_kernel, STEPS, False),
        (half, half),
        (mixing, source, middle, slope),
        [SMEM, HBM],
        20,
        scratch=[room, room] + stream,
    )
    low_rest, high_rest = exchange(up_rest, down_rest)
    middle, middle_added = march_first(change, low, high, False)
    change, change_share = call(
        change_kernel,
        (slab, share),
        (mixing, leads, source, middle, middle_added, low_rest, high_rest, slope, packed_low, packed_high),
        [SMEM, SMEM, HBM],
        50,
        scratch=march_room + [pltpu.VMEM((1,) + slab.shape, jnp.float32), room, stream[1]],
        first_out=HBM,
    )
    change_shares = lax.all_to_all(change_share, "tm", 0, 0)
    residual = jnp.where(leading, first_source, from_behind(change))
    (error_shares,) = call(scan_kernel, (share,), (mixing, slope_shares, change_shares), [SMEM], 16)
    error_share = lax.all_to_all(error_shares, "tm", 0, 0)
    corrected, middle, up, down = call(
        corrected_kernel,
        (slab, slab, half, half),
        (mixing, leads, relaxed, source, error_share, slope),
        [SMEM, SMEM, HBM, HBM],
        30,
        scratch=[room, stream[0], room, room, pltpu.SemaphoreType.DMA((STEPS + 1,))],
    )
    low, high = exchange(up, down)
    up_rest, down_rest = call(
        functools.partial(rest_kernel, STEPS - 1, True),
        (rest, rest),
        (mixing, source, middle, slope),
        [SMEM, HBM],
        16,
        scratch=[room, room] + stream,
    )
    low_rest, high_rest = exchange(up_rest, down_rest)
    states_room = march_room + [stream[0], stream[0], stream[1], stream[1]]
    later = struct(STEPS - HALF - 1, *slab.shape)
    earlier, middle, middle_added, later = call(
        states_first_kernel,
        (whole, slab, added, later),
        (mixing, source, corrected, low, high, slope, packed_low, packed_high),
        [SMEM, HBM],
        42,
        scratch=states_room,
        first_out=HBM,
    )
    (fine_states,) = call(
        states_rest_kernel,
        (whole,),
        (mixing, earlier, later, middle, middle_added, low_rest, high_rest, slope, packed_low, packed_high),
        [SMEM, HBM],
        34,
        scratch=march_room + [stream[0], stream[1]],
        first_out=HBM,
        alias={1: 0},
    )
    return fine_states, residual[None]


def solution(mesh):
    split = P("tm", None, "space", None, None)
    return jax.shard_map(
        per_device,
        mesh=mesh,
        in_specs=(split, split, split, P()),
        out_specs=(split, split),
        check_vma=False,
    )
```

```python
import functools

import jax
import jax.numpy as jnp
from jax import lax
from jax.experimental import pallas as pl
from jax.experimental.pallas import tpu as pltpu
from jax.sharding import PartitionSpec as P


STEPS = 8
FIELDS = 5
WIDE = 8
DIFFUSION = 0.1
RATE = 0.25
COARSE_STEP = 0.75
KEEP = 1.0 - 6.0 * DIFFUSION - RATE
REACH = [min(m, STEPS - 1 - m) for m in range(STEPS)]
REACH_AT = [sum(REACH[:m]) for m in range(STEPS)]
PACKED = sum(REACH)
HALF = STEPS // 2
HALO = max(min(m + 1, STEPS - 1 - m) for m in range(STEPS))


def mixed(mix, fields):
    out = []
    for i in range(FIELDS):
        total = mix[i][0] * fields[0]
        for j in range(1, FIELDS):
            total = total + mix[i][j] * fields[j]
        out.append(total)
    return out


def scalars(mix_ref):
    return [[mix_ref[i, j] for j in range(FIELDS)] for i in range(FIELDS)]


def wall_neighbours(v):
    row = lax.broadcasted_iota(jnp.int32, (8, 128), 0)
    first, last = row == 0, row == 7
    a, b = v[:8], v[8:]
    a_next, b_next = pltpu.roll(a, 1, 0), pltpu.roll(b, 1, 0)
    a_prev, b_prev = pltpu.roll(a, 7, 0), pltpu.roll(b, 7, 0)
    upper = jnp.where(first, 0.0, a_next) + jnp.where(last, b_prev, a_prev)
    lower = jnp.where(first, a_next, b_next) + jnp.where(last, 0.0, b_prev)
    return jnp.concatenate([upper, lower], axis=0)


def stepped(mix, field, beside, slope, source):
    out = []
    for f, turned in enumerate(mixed(mix, field)):
        v = field[f]
        around = pltpu.roll(v, 1, 1) + pltpu.roll(v, 127, 1) + wall_neighbours(v)
        around = around + beside[f]
        new = KEEP * v + DIFFUSION * around + slope[f] * turned
        out.append(new if source is None else new + source[f])
    return out


class Streamed:
    def __init__(self, hbm, room, sems, wanted):
        self.copies = {t: pltpu.make_async_copy(hbm.at[t], room.at[t], sems.at[t]) for t in wanted}
        for copy in self.copies.values():
            copy.start()

    def ready(self, t):
        if t in self.copies:
            self.copies.pop(t).wait()


def slopes(mix, state):
    out = []
    for value in mixed(mix, state):
        tilted = jnp.tanh(value)
        out.append(RATE - RATE * (tilted * tilted))
    return out


def border_kernel(mix_ref, primal_hbm, up_ref, down_ref, up_state, down_state, sems):
    mix = scalars(mix_ref)
    copies = []
    for m in range(STEPS):
        n, a = REACH[m], REACH_AT[m]
        if n > 0:
            ends = (pl.ds(WIDE - n, n), up_state), (pl.ds(0, n), down_state)
            for planes, state in ends:
                copies.append(
                    pltpu.make_async_copy(
                        primal_hbm.at[m, :, planes], state.at[:, a : a + n], sems.at[len(copies)]
                    )
                )
    for copy in copies:
        copy.start()
    for copy in copies:
        copy.wait()
    for state, out_ref in ((up_state, up_ref), (down_state, down_ref)):

        def plane(n, carry):
            for k in range(2):
                x = 2 * n + k
                for f, value in enumerate(slopes(mix, [state[f, x] for f in range(FIELDS)])):
                    out_ref[f, x] = value
            return carry

        lax.fori_loop(0, PACKED // 2, plane, 0)


def shares(part):
    return [(part * x + q, x, 4 * q) for x in range(WIDE) for q in range(part)]


def alone_step(mix, m, here, there, slope_ref, source_ref, ends):
    for x in range(WIDE):
        if not (x >= m + 1 or x <= WIDE - 2 - m):
            continue
        field = [here[f, x] for f in range(FIELDS)]
        if x == 0:
            beside = [here[f, 1] for f in range(FIELDS)]
        elif x == WIDE - 1:
            beside = [here[f, WIDE - 2] for f in range(FIELDS)]
        else:
            beside = [here[f, x - 1] + here[f, x + 1] for f in range(FIELDS)]
        slope = [slope_ref[m, f, x] for f in range(FIELDS)]
        source = None
        if source_ref is not None:
            source = [source_ref[m + 1, f, x] for f in range(FIELDS)]
        new = stepped(mix, field, beside, slope, source)
        for f in range(FIELDS):
            there[f, x] = new[f]
            if x == 0 or x == WIDE - 1:
                ends[(m + 1) // HALF][int(x == 0)][f, (m + 1) % HALF] = new[f]


def guess_kernel(mix_ref, primal_hbm, source_hbm, guess_ref, share_hbm, slope_ref, up_one, down_one, up_two, down_two, primal, source_ref, one, two, share_ref, sems):
    mix = scalars(mix_ref)
    primal_in = Streamed(primal_hbm, primal, sems.at[0], range(STEPS))
    source_in = Streamed(source_hbm, source_ref, sems.at[1], range(1, STEPS))
    start_ref = guess_ref.at[0]
    ends = [(up_one, down_one), (up_two, down_two)]
    for f in range(FIELDS):
        down_one[f, 0] = start_ref[f, 0]
        up_one[f, 0] = start_ref[f, WIDE - 1]
    buffers = (one, two)
    for t in range(STEPS):
        primal_in.ready(t)

        def plane(n, carry):
            for k in range(2):
                x = 2 * n + k
                state = [primal[t, f, x] for f in range(FIELDS)]
                for f, value in enumerate(slopes(mix, state)):
                    slope_ref[t, f, x] = value
            return carry

        lax.fori_loop(0, WIDE // 2, plane, 0)
        if t == 0:
            for share, x, row in shares(4):
                for f in range(FIELDS):
                    share_ref[share, f] = slope_ref[0, f, x, row : row + 4]
            share_out = pltpu.make_async_copy(share_ref, share_hbm, sems.at[1, 0])
            share_out.start()
        source_in.ready(t + 1)
        if t + 1 < STEPS:
            here = start_ref if t == 0 else buffers[t % 2]
            alone_step(mix, t, here, buffers[(t + 1) % 2], slope_ref, source_ref, ends)
    share_out.wait()


def relaxed_kernel(mix_ref, leads_ref, source_hbm, ended_ref, guess_ref, slope_ref, relaxed_hbm, change_ref, middle_ref, up_ref, down_ref, source_ref, relaxed_ref, one, two, sems):
    source_in = Streamed(source_hbm, source_ref, sems, [0])
    mix = scalars(mix_ref)
    leads = leads_ref[0] == 1
    source_in.ready(0)
    for f in range(FIELDS):
        for x in range(WIDE):
            before = guess_ref[0, f, x]
            after = jnp.where(leads, before, ended_ref[f, x] + source_ref[0, f, x])
            relaxed_ref[f, x] = after
            change_ref[f, x] = after - before
        down_ref[f, 0] = change_ref[f, 0]
        up_ref[f, 0] = change_ref[f, WIDE - 1]
    relaxed_out = pltpu.make_async_copy(relaxed_ref, relaxed_hbm, sems.at[1])
    relaxed_out.start()
    buffers = (one, two)
    for m in range(HALF - 1):
        here = change_ref if m == 0 else buffers[m % 2]
        there = middle_ref if m == HALF - 2 else buffers[(m + 1) % 2]
        alone_step(mix, m, here, there, slope_ref, None, [(up_ref, down_ref)])
    relaxed_out.wait()


def rest_kernel(count, forced, mix_ref, source_hbm, middle_ref, slope_ref, up_ref, down_ref, *rest):
    next_ref, (one, two, source_ref, sems) = rest[0], rest[-4:]
    if forced:
        fetch = pltpu.make_async_copy(source_hbm.at[1], next_ref, sems.at[0])
        fetch.start()
    source_in = Streamed(source_hbm, source_ref, sems, range(HALF, count) if forced else [])
    mix = scalars(mix_ref)
    buffers = (one, two)
    for m in range(HALF - 1, count - 1):
        source_in.ready(m + 1)
        here = middle_ref if m == HALF - 1 else buffers[m % 2]
        source = source_ref if forced else None
        alone_step(mix, m, here, buffers[(m + 1) % 2], slope_ref, source, [None, (up_ref, down_ref)])
    if forced:
        fetch.wait()


def corrected_kernel(mix_ref, leads_ref, relaxed_hbm, source_hbm, share_ref, slope_ref, corrected_ref, middle_ref, up_ref, down_ref, relaxed_ref, source_ref, one, two, sems):
    relaxed_in = pltpu.make_async_copy(relaxed_hbm, relaxed_ref, sems.at[STEPS])
    relaxed_in.start()
    source_in = Streamed(source_hbm, source_ref, sems, range(HALF))
    mix = scalars(mix_ref)
    leads = leads_ref[0] == 1
    relaxed_in.wait()
    source_in.ready(0)
    for share, x, row in shares(4):
        for f in range(FIELDS):
            rows = slice(row, row + 4)
            error = jnp.where(leads, source_ref[0, f, x, rows], share_ref[share, f])
            corrected_ref[f, x, rows] = relaxed_ref[f, x, rows] + error
    for f in range(FIELDS):
        down_ref[f, 0] = corrected_ref[f, 0]
        up_ref[f, 0] = corrected_ref[f, WIDE - 1]
    buffers = (one, two)
    for m in range(HALF - 1):
        source_in.ready(m + 1)
        here = corrected_ref if m == 0 else buffers[m % 2]
        there = middle_ref if m == HALF - 2 else buffers[(m + 1) % 2]
        alone_step(mix, m, here, there, slope_ref, source_ref, [(up_ref, down_ref)])


def march_steps(count, steps, forced, done, step_opens, step_ends, mix, start_ref, start_added, low_ref, high_ref, slope_ref, source_ref, packed_low, packed_high, one, two, added_one, added_two, middle=None):
    fields = range(FIELDS)
    buffers, extras = (one, two), (added_one, added_two)
    sides = (
        (0, low_ref, packed_low, lambda n, p: n - p),
        (WIDE - 1, high_ref, packed_high, lambda n, p: p - 1),
    )
    for m in steps:
        here = start_ref if m == steps[0] else buffers[m % 2]
        step_opens(m)
        here_added = start_added if m == steps[0] else extras[m % 2]
        there, there_added = buffers[(m + 1) % 2], extras[(m + 1) % 2]
        if middle is not None and m == steps[-1]:
            there, there_added = middle
        last = m + 1 == count

        def own(x, beside):
            field = [here[f, x] for f in fields]
            slope = [slope_ref[m, f, x] for f in fields]
            source = [source_ref[m + 1, f, x] for f in fields] if forced and m + 1 < STEPS else None
            new = stepped(mix, field, beside, slope, source)
            for f in fields:
                if not last:
                    there[f, x] = new[f]
                done(m + 1, f, x, new[f])

        for side, (edge, alone, packed, place) in enumerate(sides):
            inner = edge + 1 if edge == 0 else edge - 1
            beyond = [alone[m // HALF][f, m % HALF] for f in fields]
            if m > 0:
                beyond = [beyond[f] + here_added[side, f, 0] for f in fields]
            own(edge, [here[f, inner] + beyond[f] for f in fields])
            for p in range(1, min(m + 1, count - 1 - m) + 1):
                nearer = [here[f, edge] if p == 1 else here_added[side, f, p - 2] for f in fields]
                if p == m + 1:
                    for f in fields:
                        there_added[side, f, p - 1] = DIFFUSION * nearer[f]
                    continue
                beside = nearer
                if p + 1 <= m:
                    beside = [nearer[f] + here_added[side, f, p] for f in fields]
                at = REACH_AT[m] + place(REACH[m], p)
                new = stepped(
                    mix,
                    [here_added[side, f, p - 1] for f in fields],
                    beside,
                    [packed[f, at] for f in fields],
                    None,
                )
                for f in fields:
                    there_added[side, f, p - 1] = new[f]

        def inside(i, carry):
            for k in range(3):
                x = 1 + 3 * i + k
                own(x, [here[f, x - 1] + here[f, x + 1] for f in fields])
            return carry

        lax.fori_loop(0, 2, inside, 0)
        step_ends(m)


def nothing(m):
    pass


def march_first_kernel(count, forced, mix_ref, source_hbm, start_ref, low_ref, high_ref, slope_ref, packed_low, packed_high, middle_ref, middle_added, *rest):
    later_ref, (one, two, added_one, added_two, source_ref, sems) = rest[0], rest[-6:]
    source_in = Streamed(source_hbm, source_ref, sems, range(1, HALF + 1) if forced else [])
    later = pltpu.make_async_copy(source_hbm.at[HALF + 1 :], later_ref, sems.at[HALF + 1]) if forced else None
    if forced:
        later.start()
    march_steps(
        count, range(HALF), forced, lambda *_: None, lambda m: source_in.ready(m + 1), nothing, scalars(mix_ref),
        start_ref, None, (low_ref, None), (high_ref, None), slope_ref, source_ref, packed_low, packed_high,
        one, two, added_one, added_two, (middle_ref, middle_added),
    )
    if forced:
        later.wait()


class Parts:
    def __init__(self, parts):
        self.parts = parts

    def __getitem__(self, index):
        return self.parts[index[0]][index[1:]]


def later_parts(ref):
    return {t: ref.at[t - HALF - 1] for t in range(HALF + 1, STEPS)}


def end_kernel(mix_ref, later_ref, middle_ref, middle_added, low_ref, high_ref, slope_ref, packed_low, packed_high, out_ref, one, two, added_one, added_two):
    def done(step, f, x, value):
        if step == STEPS:
            out_ref[f, x] = value

    march_steps(
        STEPS, range(HALF, STEPS), True, done, nothing, nothing, scalars(mix_ref),
        middle_ref, middle_added, (None, low_ref), (None, high_ref), slope_ref, Parts(later_parts(later_ref)), packed_low, packed_high,
        one, two, added_one, added_two,
    )


def change_kernel(mix_ref, leads_ref, source_hbm, middle_ref, middle_added, low_ref, high_ref, slope_ref, packed_low, packed_high, out_hbm, share_ref, one, two, added_one, added_two, source_ref, out_ref, sems):
    source_in = Streamed(source_hbm, source_ref, sems, [0])
    mix = scalars(mix_ref)

    def done(step, f, x, value):
        if step == STEPS:
            out_ref[f, x] = value

    march_steps(
        STEPS, range(HALF, STEPS), False, done, nothing, nothing, mix,
        middle_ref, middle_added, (None, low_ref), (None, high_ref), slope_ref, None, packed_low, packed_high,
        one, two, added_one, added_two,
    )
    out = pltpu.make_async_copy(out_ref, out_hbm, sems.at[1])
    out.start()
    for share, x, row in shares(4):
        for f in range(FIELDS):
            share_ref[share, f] = out_ref[f, x, row : row + 4]
    source_in.ready(0)

    @pl.when(leads_ref[0] == 1)
    def _():
        for x in range(WIDE):
            error = [source_ref[0, f, x] for f in range(FIELDS)]
            slope = [slope_ref[0, f, x] for f in range(FIELDS)]
            for f, moved in enumerate(coarse_turn(mix, error, slope)):
                value = moved + out_ref[f, x]
                for q in range(4):
                    share_ref[4 * x + q, f] = value[4 * q : 4 * q + 4]

    out.wait()


def states_first_kernel(mix_ref, source_hbm, next_ref, start_ref, low_ref, high_ref, slope_ref, packed_low, packed_high, out_hbm, middle_ref, middle_added, later_ref, one, two, added_one, added_two, source_ref, out_ref, sems, out_sems):
    source_in = Streamed(source_hbm, source_ref, sems, range(2, HALF + 1))
    parts = {1: next_ref} | {t: source_ref.at[t] for t in range(2, HALF + 1)}
    later = pltpu.make_async_copy(source_hbm.at[HALF + 1 :], later_ref, sems.at[HALF + 1])
    later.start()
    outs = [
        pltpu.make_async_copy(start_ref if t == 0 else out_ref.at[t], out_hbm.at[t], out_sems.at[t])
        for t in range(HALF)
    ]
    outs[0].start()

    def done(step, f, x, value):
        if step < HALF:
            out_ref[step, f, x] = value

    march_steps(
        STEPS - 1, range(HALF), True, done, lambda m: source_in.ready(m + 1), lambda m: outs[m + 1].start() if m + 1 < HALF else None,
        scalars(mix_ref),
        start_ref, None, (low_ref, None), (high_ref, None), slope_ref, Parts(parts), packed_low, packed_high,
        one, two, added_one, added_two, (middle_ref, middle_added),
    )
    later.wait()
    for out in outs:
        out.wait()


def states_rest_kernel(mix_ref, earlier_hbm, later_ref, middle_ref, middle_added, low_ref, high_ref, slope_ref, packed_low, packed_high, out_hbm, one, two, added_one, added_two, out_ref, out_sems):
    outs = {
        t: pltpu.make_async_copy(middle_ref if t == HALF else out_ref.at[t], out_hbm.at[t], out_sems.at[t])
        for t in range(HALF, STEPS)
    }
    outs[HALF].start()

    def done(step, f, x, value):
        out_ref[step, f, x] = value

    march_steps(
        STEPS - 1, range(HALF, STEPS - 1), True, done, nothing, lambda m: outs[m + 1].start(), scalars(mix_ref),
        middle_ref, middle_added, (None, low_ref), (None, high_ref), slope_ref, Parts(later_parts(later_ref)),
        packed_low, packed_high, one, two, added_one, added_two,
    )
    for out in outs.values():
        out.wait()


def coarse_turn(mix, error, slope):
    out = []
    for f, turned in enumerate(mixed(mix, error)):
        out.append((1.0 - COARSE_STEP) * error[f] + (COARSE_STEP / RATE) * slope[f] * turned)
    return out


def scan_kernel(mix_ref, slope_ref, resid_ref, error_ref):
    mix = scalars(mix_ref)
    blocks = resid_ref.shape[0]
    error = tuple(resid_ref[0, f] for f in range(FIELDS))
    for f in range(FIELDS):
        error_ref[0, f] = error[f]
        error_ref[1, f] = error[f]

    def turn(i, error):
        moved = coarse_turn(mix, error, [slope_ref[i, f] for f in range(FIELDS)])
        new = tuple(moved[f] + resid_ref[i, f] for f in range(FIELDS))
        for f in range(FIELDS):
            error_ref[i + 1, f] = new[f]
        return new

    lax.fori_loop(1, blocks - 1, turn, error, unroll=3 if (blocks - 2) % 3 == 0 else 1)


VMEM = pl.BlockSpec(memory_space=pltpu.VMEM)
SMEM = pl.BlockSpec(memory_space=pltpu.SMEM)
HBM = pl.BlockSpec(memory_space=pltpu.HBM)


def call(kernel, out, operands, places, planes, scratch=(), first_out=None, alias=None):
    read = sum(4 * operand.size for operand in operands)
    written = sum(4 * leaf.size for leaf in jax.tree.leaves(out))
    if first_out is not None:
        out = (pltpu.HBM(out[0].shape, out[0].dtype),) + tuple(out[1:])
    return pl.pallas_call(
        kernel,
        input_output_aliases=alias or {},
        out_shape=out,
        in_specs=places + [VMEM] * (len(operands) - len(places)),
        out_specs=[first_out or VMEM] + [VMEM] * (len(out) - 1),
        scratch_shapes=list(scratch),
        compiler_params=pltpu.CompilerParams(vmem_limit_bytes=20 << 20),
        cost_estimate=pl.CostEstimate(
            flops=planes * FIELDS * 2048 * 25, bytes_accessed=read + written, transcendentals=0
        ),
    )(*operands)


def in_hbm(array):
    return pltpu.with_memory_space_constraint(array, pltpu.HBM)


def struct(*shape):
    return jax.ShapeDtypeStruct(shape, jnp.float32)


def from_behind(array):
    count = lax.axis_size("tm")
    return lax.ppermute(array, "tm", [(i, i + 1) for i in range(count - 1)])


def exchange(up, down):
    count = lax.axis_size("space")
    forward = [(i, (i + 1) % count) for i in range(count)]
    backward = [(b, a) for a, b in forward]
    return lax.ppermute(up, "space", forward), lax.ppermute(down, "space", backward)


def per_device(primal, source, guess, mixing):
    parts = lax.axis_size("tm")
    leading = lax.axis_index("tm") == 0
    leads = leading.astype(jnp.int32)[None]
    plane = primal.shape[3:]
    slab = struct(*primal.shape[1:])
    whole = struct(*primal.shape)
    share = struct(parts, FIELDS, 4, plane[1])
    room = pltpu.VMEM(slab.shape, jnp.float32)
    extra = pltpu.VMEM((2, FIELDS, HALO) + plane, jnp.float32)
    march_room = [room, room, extra, extra]
    packed = struct(FIELDS, PACKED, *plane)

    packed_room = pltpu.VMEM(packed.shape, jnp.float32)
    up, down = call(
        border_kernel,
        (packed, packed),
        (in_hbm(mixing), in_hbm(primal)),
        [SMEM, HBM],
        2 * PACKED,
        scratch=[packed_room, packed_room, pltpu.SemaphoreType.DMA((2 * STEPS,))],
    )
    packed_low, packed_high = exchange(up, down)
    first_source = source[0]
    primal, source = in_hbm(primal), in_hbm(source)
    stream = [pltpu.VMEM(whole.shape, jnp.float32), pltpu.SemaphoreType.DMA((STEPS,))]
    half, rest = struct(FIELDS, HALF, *plane), struct(FIELDS, HALF - 1, *plane)
    added = struct(2, FIELDS, HALO, *plane)

    def march_first(start, low, high, forced):
        later = (struct(STEPS - HALF - 1, *slab.shape),) if forced else ()
        return call(
            functools.partial(march_first_kernel, STEPS, forced),
            (slab, added) + later,
            (mixing, source, start, low, high, slope, packed_low, packed_high),
            [SMEM, HBM],
            42,
            scratch=march_room + stream,
        )

    slope_share, slope, up, down, up_rest, down_rest = call(
        guess_kernel,
        (share, whole, half, half, half, half),
        (mixing, primal, source, guess),
        [SMEM, HBM, HBM],
        100,
        scratch=[stream[0], stream[0], room, room, pltpu.VMEM(share.shape, jnp.float32), pltpu.SemaphoreType.DMA((2, STEPS))],
        first_out=HBM,
    )
    low, high = exchange(up, down)
    low_rest, high_rest = exchange(up_rest, down_rest)
    middle, middle_added, later = march_first(guess[0], low, high, True)
    (ended,) = call(
        end_kernel,
        (slab,),
        (mixing, later, middle, middle_added, low_rest, high_rest, slope, packed_low, packed_high),
        [SMEM],
        46,
        scratch=march_room,
    )
    ended = from_behind(ended)
    slope_shares = lax.all_to_all(slope_share, "tm", 0, 0)
    relaxed, change, middle, up, down = call(
        relaxed_kernel,
        (slab, slab, slab, half, half),
        (mixing, leads, source, ended, guess, slope),
        [SMEM, SMEM, HBM],
        30,
        scratch=[pltpu.VMEM((1,) + slab.shape, jnp.float32), room, room, room, stream[1]],
        first_out=HBM,
    )
    low, high = exchange(up, down)
    up_rest, down_rest = call(
        functools.partial(rest_kernel, STEPS, False),
        (half, half),
        (mixing, source, middle, slope),
        [SMEM, HBM],
        20,
        scratch=[room, room] + stream,
    )
    low_rest, high_rest = exchange(up_rest, down_rest)
    middle, middle_added = march_first(change, low, high, False)
    change, change_share = call(
        change_kernel,
        (slab, share),
        (mixing, leads, source, middle, middle_added, low_rest, high_rest, slope, packed_low, packed_high),
        [SMEM, SMEM, HBM],
        50,
        scratch=march_room + [pltpu.VMEM((1,) + slab.shape, jnp.float32), room, stream[1]],
        first_out=HBM,
    )
    change_shares = lax.all_to_all(change_share, "tm", 0, 0)
    residual = jnp.where(leading, first_source, from_behind(change))
    (error_shares,) = call(scan_kernel, (share,), (mixing, slope_shares, change_shares), [SMEM], 16)
    error_share = lax.all_to_all(error_shares, "tm", 0, 0)
    corrected, middle, up, down = call(
        corrected_kernel,
        (slab, slab, half, half),
        (mixing, leads, in_hbm(relaxed), source, error_share, slope),
        [SMEM, SMEM, HBM, HBM],
        30,
        scratch=[room, stream[0], room, room, pltpu.SemaphoreType.DMA((STEPS + 1,))],
    )
    low, high = exchange(up, down)
    up_rest, down_rest, upcoming = call(
        functools.partial(rest_kernel, STEPS - 1, True),
        (rest, rest, slab),
        (mixing, source, middle, slope),
        [SMEM, HBM],
        16,
        scratch=[room, room] + stream,
    )
    low_rest, high_rest = exchange(up_rest, down_rest)
    states_room = march_room + [stream[0], stream[0], stream[1], stream[1]]
    later = struct(STEPS - HALF - 1, *slab.shape)
    earlier, middle, middle_added, later = call(
        states_first_kernel,
        (whole, slab, added, later),
        (mixing, source, upcoming, corrected, low, high, slope, packed_low, packed_high),
        [SMEM, HBM],
        42,
        scratch=states_room,
        first_out=HBM,
    )
    (fine_states,) = call(
        states_rest_kernel,
        (whole,),
        (mixing, earlier, later, middle, middle_added, low_rest, high_rest, slope, packed_low, packed_high),
        [SMEM, HBM],
        34,
        scratch=march_room + [stream[0], stream[1]],
        first_out=HBM,
        alias={1: 0},
    )
    return fine_states, residual[None]


def solution(mesh):
    split = P("tm", None, "space", None, None)
    return jax.shard_map(
        per_device,
        mesh=mesh,
        in_specs=(split, split, split, P()),
        out_specs=(split, split),
        check_vma=False,
    )
```

```python
import functools

import jax
import jax.numpy as jnp
from jax import lax
from jax.experimental import pallas as pl
from jax.experimental.pallas import tpu as pltpu
from jax.sharding import PartitionSpec as P


STEPS = 8
FIELDS = 5
WIDE = 8
DIFFUSION = 0.1
RATE = 0.25
COARSE_STEP = 0.75
KEEP = 1.0 - 6.0 * DIFFUSION - RATE
REACH = [min(m, STEPS - 1 - m) for m in range(STEPS)]
REACH_AT = [sum(REACH[:m]) for m in range(STEPS)]
PACKED = sum(REACH)
HALF = 5
HALO = max(min(m + 1, STEPS - 1 - m) for m in range(STEPS))


def mixed(mix, fields):
    out = []
    for i in range(FIELDS):
        total = mix[i][0] * fields[0]
        for j in range(1, FIELDS):
            total = total + mix[i][j] * fields[j]
        out.append(total)
    return out


def scalars(mix_ref):
    return [[mix_ref[i, j] for j in range(FIELDS)] for i in range(FIELDS)]


def wall_neighbours(v):
    row = lax.broadcasted_iota(jnp.int32, (8, 128), 0)
    first, last = row == 0, row == 7
    a, b = v[:8], v[8:]
    a_next, b_next = pltpu.roll(a, 1, 0), pltpu.roll(b, 1, 0)
    a_prev, b_prev = pltpu.roll(a, 7, 0), pltpu.roll(b, 7, 0)
    upper = jnp.where(first, 0.0, a_next) + jnp.where(last, b_prev, a_prev)
    lower = jnp.where(first, a_next, b_next) + jnp.where(last, 0.0, b_prev)
    return jnp.concatenate([upper, lower], axis=0)


def stepped(mix, field, beside, slope, source):
    out = []
    for f, turned in enumerate(mixed(mix, field)):
        v = field[f]
        around = pltpu.roll(v, 1, 1) + pltpu.roll(v, 127, 1) + wall_neighbours(v)
        around = around + beside[f]
        new = KEEP * v + DIFFUSION * around + slope[f] * turned
        out.append(new if source is None else new + source[f])
    return out


class Streamed:
    def __init__(self, hbm, room, sems, wanted):
        self.copies = {t: pltpu.make_async_copy(hbm.at[t], room.at[t], sems.at[t]) for t in wanted}
        for copy in self.copies.values():
            copy.start()

    def ready(self, t):
        if t in self.copies:
            self.copies.pop(t).wait()


def slopes(mix, state):
    out = []
    for value in mixed(mix, state):
        tilted = jnp.tanh(value)
        out.append(RATE - RATE * (tilted * tilted))
    return out


def border_kernel(mix_ref, primal_hbm, up_ref, down_ref, up_state, down_state, sems):
    mix = scalars(mix_ref)
    copies = []
    for m in range(STEPS):
        n, a = REACH[m], REACH_AT[m]
        if n > 0:
            ends = (pl.ds(WIDE - n, n), up_state), (pl.ds(0, n), down_state)
            for planes, state in ends:
                copies.append(
                    pltpu.make_async_copy(
                        primal_hbm.at[m, :, planes], state.at[:, a : a + n], sems.at[len(copies)]
                    )
                )
    for copy in copies:
        copy.start()
    for copy in copies:
        copy.wait()
    for state, out_ref in ((up_state, up_ref), (down_state, down_ref)):

        def plane(n, carry):
            for k in range(2):
                x = 2 * n + k
                for f, value in enumerate(slopes(mix, [state[f, x] for f in range(FIELDS)])):
                    out_ref[f, x] = value
            return carry

        lax.fori_loop(0, PACKED // 2, plane, 0)


def shares(part):
    return [(part * x + q, x, 4 * q) for x in range(WIDE) for q in range(part)]


def alone_step(mix, m, here, there, slope_ref, source_ref, ends):
    for x in range(WIDE):
        if not (x >= m + 1 or x <= WIDE - 2 - m):
            continue
        field = [here[f, x] for f in range(FIELDS)]
        if x == 0:
            beside = [here[f, 1] for f in range(FIELDS)]
        elif x == WIDE - 1:
            beside = [here[f, WIDE - 2] for f in range(FIELDS)]
        else:
            beside = [here[f, x - 1] + here[f, x + 1] for f in range(FIELDS)]
        slope = [slope_ref[m, f, x] for f in range(FIELDS)]
        source = None
        if source_ref is not None:
            source = [source_ref[m + 1, f, x] for f in range(FIELDS)]
        new = stepped(mix, field, beside, slope, source)
        for f in range(FIELDS):
            there[f, x] = new[f]
            if x == 0 or x == WIDE - 1:
                ends[(m + 1) // HALF][int(x == 0)][f, (m + 1) % HALF] = new[f]


def guess_kernel(mix_ref, primal_hbm, source_hbm, guess_ref, share_hbm, slope_ref, up_one, down_one, up_two, down_two, primal, source_ref, one, two, share_ref, sems):
    mix = scalars(mix_ref)
    primal_in = Streamed(primal_hbm, primal, sems.at[0], range(STEPS))
    source_in = Streamed(source_hbm, source_ref, sems.at[1], range(1, STEPS))
    start_ref = guess_ref.at[0]
    ends = [(up_one, down_one), (up_two, down_two)]
    for f in range(FIELDS):
        down_one[f, 0] = start_ref[f, 0]
        up_one[f, 0] = start_ref[f, WIDE - 1]
    buffers = (one, two)
    for t in range(STEPS):
        primal_in.ready(t)

        def plane(n, carry):
            for k in range(2):
                x = 2 * n + k
                state = [primal[t, f, x] for f in range(FIELDS)]
                for f, value in enumerate(slopes(mix, state)):
                    slope_ref[t, f, x] = value
            return carry

        lax.fori_loop(0, WIDE // 2, plane, 0)
        if t == 0:
            for share, x, row in shares(4):
                for f in range(FIELDS):
                    share_ref[share, f] = slope_ref[0, f, x, row : row + 4]
            share_out = pltpu.make_async_copy(share_ref, share_hbm, sems.at[1, 0])
            share_out.start()
        source_in.ready(t + 1)
        if t + 1 < STEPS:
            here = start_ref if t == 0 else buffers[t % 2]
            alone_step(mix, t, here, buffers[(t + 1) % 2], slope_ref, source_ref, ends)
    share_out.wait()


def relaxed_kernel(mix_ref, leads_ref, source_hbm, ended_ref, guess_ref, slope_ref, relaxed_hbm, change_ref, middle_ref, up_ref, down_ref, source_ref, relaxed_ref, one, two, sems):
    source_in = Streamed(source_hbm, source_ref, sems, [0])
    mix = scalars(mix_ref)
    leads = leads_ref[0] == 1
    source_in.ready(0)
    for f in range(FIELDS):
        for x in range(WIDE):
            before = guess_ref[0, f, x]
            after = jnp.where(leads, before, ended_ref[f, x] + source_ref[0, f, x])
            relaxed_ref[f, x] = after
            change_ref[f, x] = after - before
        down_ref[f, 0] = change_ref[f, 0]
        up_ref[f, 0] = change_ref[f, WIDE - 1]
    relaxed_out = pltpu.make_async_copy(relaxed_ref, relaxed_hbm, sems.at[1])
    relaxed_out.start()
    buffers = (one, two)
    for m in range(HALF - 1):
        here = change_ref if m == 0 else buffers[m % 2]
        there = middle_ref if m == HALF - 2 else buffers[(m + 1) % 2]
        alone_step(mix, m, here, there, slope_ref, None, [(up_ref, down_ref)])
    relaxed_out.wait()


def rest_kernel(count, forced, mix_ref, source_hbm, middle_ref, slope_ref, up_ref, down_ref, *rest):
    next_ref, (one, two, source_ref, sems) = rest[0], rest[-4:]
    if forced:
        fetch = pltpu.make_async_copy(source_hbm.at[1], next_ref, sems.at[0])
        fetch.start()
    source_in = Streamed(source_hbm, source_ref, sems, range(HALF, count) if forced else [])
    mix = scalars(mix_ref)
    buffers = (one, two)
    for m in range(HALF - 1, count - 1):
        source_in.ready(m + 1)
        here = middle_ref if m == HALF - 1 else buffers[m % 2]
        source = source_ref if forced else None
        alone_step(mix, m, here, buffers[(m + 1) % 2], slope_ref, source, [None, (up_ref, down_ref)])
    if forced:
        fetch.wait()


def corrected_kernel(mix_ref, leads_ref, relaxed_hbm, source_hbm, share_ref, slope_ref, corrected_ref, middle_ref, up_ref, down_ref, relaxed_ref, source_ref, one, two, sems):
    relaxed_in = pltpu.make_async_copy(relaxed_hbm, relaxed_ref, sems.at[STEPS])
    relaxed_in.start()
    source_in = Streamed(source_hbm, source_ref, sems, range(HALF))
    mix = scalars(mix_ref)
    leads = leads_ref[0] == 1
    relaxed_in.wait()
    source_in.ready(0)
    for share, x, row in shares(4):
        for f in range(FIELDS):
            rows = slice(row, row + 4)
            error = jnp.where(leads, source_ref[0, f, x, rows], share_ref[share, f])
            corrected_ref[f, x, rows] = relaxed_ref[f, x, rows] + error
    for f in range(FIELDS):
        down_ref[f, 0] = corrected_ref[f, 0]
        up_ref[f, 0] = corrected_ref[f, WIDE - 1]
    buffers = (one, two)
    for m in range(HALF - 1):
        source_in.ready(m + 1)
        here = corrected_ref if m == 0 else buffers[m % 2]
        there = middle_ref if m == HALF - 2 else buffers[(m + 1) % 2]
        alone_step(mix, m, here, there, slope_ref, source_ref, [(up_ref, down_ref)])


def march_steps(count, steps, forced, done, step_opens, step_ends, mix, start_ref, start_added, low_ref, high_ref, slope_ref, source_ref, packed_low, packed_high, one, two, added_one, added_two, middle=None):
    fields = range(FIELDS)
    buffers, extras = (one, two), (added_one, added_two)
    sides = (
        (0, low_ref, packed_low, lambda n, p: n - p),
        (WIDE - 1, high_ref, packed_high, lambda n, p: p - 1),
    )
    for m in steps:
        here = start_ref if m == steps[0] else buffers[m % 2]
        step_opens(m)
        here_added = start_added if m == steps[0] else extras[m % 2]
        there, there_added = buffers[(m + 1) % 2], extras[(m + 1) % 2]
        if middle is not None and m == steps[-1]:
            there, there_added = middle
        last = m + 1 == count

        def own(x, beside):
            field = [here[f, x] for f in fields]
            slope = [slope_ref[m, f, x] for f in fields]
            source = [source_ref[m + 1, f, x] for f in fields] if forced and m + 1 < STEPS else None
            new = stepped(mix, field, beside, slope, source)
            for f in fields:
                if not last:
                    there[f, x] = new[f]
                done(m + 1, f, x, new[f])

        for side, (edge, alone, packed, place) in enumerate(sides):
            inner = edge + 1 if edge == 0 else edge - 1
            beyond = [alone[m // HALF][f, m % HALF] for f in fields]
            if m > 0:
                beyond = [beyond[f] + here_added[side, f, 0] for f in fields]
            own(edge, [here[f, inner] + beyond[f] for f in fields])
            for p in range(1, min(m + 1, count - 1 - m) + 1):
                nearer = [here[f, edge] if p == 1 else here_added[side, f, p - 2] for f in fields]
                if p == m + 1:
                    for f in fields:
                        there_added[side, f, p - 1] = DIFFUSION * nearer[f]
                    continue
                beside = nearer
                if p + 1 <= m:
                    beside = [nearer[f] + here_added[side, f, p] for f in fields]
                at = REACH_AT[m] + place(REACH[m], p)
                new = stepped(
                    mix,
                    [here_added[side, f, p - 1] for f in fields],
                    beside,
                    [packed[f, at] for f in fields],
                    None,
                )
                for f in fields:
                    there_added[side, f, p - 1] = new[f]

        def inside(i, carry):
            for k in range(3):
                x = 1 + 3 * i + k
                own(x, [here[f, x - 1] + here[f, x + 1] for f in fields])
            return carry

        lax.fori_loop(0, 2, inside, 0)
        step_ends(m)


def nothing(m):
    pass


def march_first_kernel(count, forced, mix_ref, source_hbm, start_ref, low_ref, high_ref, slope_ref, packed_low, packed_high, middle_ref, middle_added, *rest):
    later_ref, (one, two, added_one, added_two, source_ref, sems) = rest[0], rest[-6:]
    source_in = Streamed(source_hbm, source_ref, sems, range(1, HALF + 1) if forced else [])
    later = pltpu.make_async_copy(source_hbm.at[HALF + 1 :], later_ref, sems.at[HALF + 1]) if forced else None
    if forced:
        later.start()
    march_steps(
        count, range(HALF), forced, lambda *_: None, lambda m: source_in.ready(m + 1), nothing, scalars(mix_ref),
        start_ref, None, (low_ref, None), (high_ref, None), slope_ref, source_ref, packed_low, packed_high,
        one, two, added_one, added_two, (middle_ref, middle_added),
    )
    if forced:
        later.wait()


class Parts:
    def __init__(self, parts):
        self.parts = parts

    def __getitem__(self, index):
        return self.parts[index[0]][index[1:]]


def later_parts(ref):
    return {t: ref.at[t - HALF - 1] for t in range(HALF + 1, STEPS)}


def end_kernel(mix_ref, later_ref, middle_ref, middle_added, low_ref, high_ref, slope_ref, packed_low, packed_high, out_ref, one, two, added_one, added_two):
    def done(step, f, x, value):
        if step == STEPS:
            out_ref[f, x] = value

    march_steps(
        STEPS, range(HALF, STEPS), True, done, nothing, nothing, scalars(mix_ref),
        middle_ref, middle_added, (None, low_ref), (None, high_ref), slope_ref, Parts(later_parts(later_ref)), packed_low, packed_high,
        one, two, added_one, added_two,
    )


def change_kernel(mix_ref, leads_ref, source_hbm, middle_ref, middle_added, low_ref, high_ref, slope_ref, packed_low, packed_high, out_hbm, share_ref, one, two, added_one, added_two, source_ref, out_ref, sems):
    source_in = Streamed(source_hbm, source_ref, sems, [0])
    mix = scalars(mix_ref)

    def done(step, f, x, value):
        if step == STEPS:
            out_ref[f, x] = value

    march_steps(
        STEPS, range(HALF, STEPS), False, done, nothing, nothing, mix,
        middle_ref, middle_added, (None, low_ref), (None, high_ref), slope_ref, None, packed_low, packed_high,
        one, two, added_one, added_two,
    )
    out = pltpu.make_async_copy(out_ref, out_hbm, sems.at[1])
    out.start()
    for share, x, row in shares(4):
        for f in range(FIELDS):
            share_ref[share, f] = out_ref[f, x, row : row + 4]
    source_in.ready(0)

    @pl.when(leads_ref[0] == 1)
    def _():
        for x in range(WIDE):
            error = [source_ref[0, f, x] for f in range(FIELDS)]
            slope = [slope_ref[0, f, x] for f in range(FIELDS)]
            for f, moved in enumerate(coarse_turn(mix, error, slope)):
                value = moved + out_ref[f, x]
                for q in range(4):
                    share_ref[4 * x + q, f] = value[4 * q : 4 * q + 4]

    out.wait()


def states_first_kernel(mix_ref, source_hbm, next_ref, start_ref, low_ref, high_ref, slope_ref, packed_low, packed_high, out_hbm, middle_ref, middle_added, later_ref, one, two, added_one, added_two, source_ref, out_ref, sems, out_sems):
    source_in = Streamed(source_hbm, source_ref, sems, range(2, HALF + 1))
    parts = {1: next_ref} | {t: source_ref.at[t] for t in range(2, HALF + 1)}
    later = pltpu.make_async_copy(source_hbm.at[HALF + 1 :], later_ref, sems.at[HALF + 1])
    later.start()
    outs = [
        pltpu.make_async_copy(start_ref if t == 0 else out_ref.at[t], out_hbm.at[t], out_sems.at[t])
        for t in range(HALF)
    ]
    outs[0].start()

    def done(step, f, x, value):
        if step < HALF:
            out_ref[step, f, x] = value

    march_steps(
        STEPS - 1, range(HALF), True, done, lambda m: source_in.ready(m + 1), lambda m: outs[m + 1].start() if m + 1 < HALF else None,
        scalars(mix_ref),
        start_ref, None, (low_ref, None), (high_ref, None), slope_ref, Parts(parts), packed_low, packed_high,
        one, two, added_one, added_two, (middle_ref, middle_added),
    )
    later.wait()
    for out in outs:
        out.wait()


def states_rest_kernel(mix_ref, earlier_hbm, later_ref, middle_ref, middle_added, low_ref, high_ref, slope_ref, packed_low, packed_high, out_hbm, one, two, added_one, added_two, out_ref, out_sems):
    outs = {
        t: pltpu.make_async_copy(middle_ref if t == HALF else out_ref.at[t], out_hbm.at[t], out_sems.at[t])
        for t in range(HALF, STEPS)
    }
    outs[HALF].start()

    def done(step, f, x, value):
        out_ref[step, f, x] = value

    march_steps(
        STEPS - 1, range(HALF, STEPS - 1), True, done, nothing, lambda m: outs[m + 1].start(), scalars(mix_ref),
        middle_ref, middle_added, (None, low_ref), (None, high_ref), slope_ref, Parts(later_parts(later_ref)),
        packed_low, packed_high, one, two, added_one, added_two,
    )
    for out in outs.values():
        out.wait()


def coarse_turn(mix, error, slope):
    out = []
    for f, turned in enumerate(mixed(mix, error)):
        out.append((1.0 - COARSE_STEP) * error[f] + (COARSE_STEP / RATE) * slope[f] * turned)
    return out


def scan_kernel(mix_ref, slope_ref, resid_ref, error_ref):
    mix = scalars(mix_ref)
    blocks = resid_ref.shape[0]
    error = tuple(resid_ref[0, f] for f in range(FIELDS))
    for f in range(FIELDS):
        error_ref[0, f] = error[f]
        error_ref[1, f] = error[f]

    def turn(i, error):
        moved = coarse_turn(mix, error, [slope_ref[i, f] for f in range(FIELDS)])
        new = tuple(moved[f] + resid_ref[i, f] for f in range(FIELDS))
        for f in range(FIELDS):
            error_ref[i + 1, f] = new[f]
        return new

    lax.fori_loop(1, blocks - 1, turn, error, unroll=3 if (blocks - 2) % 3 == 0 else 1)


VMEM = pl.BlockSpec(memory_space=pltpu.VMEM)
SMEM = pl.BlockSpec(memory_space=pltpu.SMEM)
HBM = pl.BlockSpec(memory_space=pltpu.HBM)


def call(kernel, out, operands, places, planes, scratch=(), first_out=None, alias=None):
    read = sum(4 * operand.size for operand in operands)
    written = sum(4 * leaf.size for leaf in jax.tree.leaves(out))
    if first_out is not None:
        out = (pltpu.HBM(out[0].shape, out[0].dtype),) + tuple(out[1:])
    return pl.pallas_call(
        kernel,
        input_output_aliases=alias or {},
        out_shape=out,
        in_specs=places + [VMEM] * (len(operands) - len(places)),
        out_specs=[first_out or VMEM] + [VMEM] * (len(out) - 1),
        scratch_shapes=list(scratch),
        compiler_params=pltpu.CompilerParams(vmem_limit_bytes=20 << 20),
        cost_estimate=pl.CostEstimate(
            flops=planes * FIELDS * 2048 * 25, bytes_accessed=read + written, transcendentals=0
        ),
    )(*operands)


def in_hbm(array):
    return pltpu.with_memory_space_constraint(array, pltpu.HBM)


def struct(*shape):
    return jax.ShapeDtypeStruct(shape, jnp.float32)


def from_behind(array):
    count = lax.axis_size("tm")
    return lax.ppermute(array, "tm", [(i, i + 1) for i in range(count - 1)])


def exchange(up, down):
    count = lax.axis_size("space")
    forward = [(i, (i + 1) % count) for i in range(count)]
    backward = [(b, a) for a, b in forward]
    return lax.ppermute(up, "space", forward), lax.ppermute(down, "space", backward)


def per_device(primal, source, guess, mixing):
    parts = lax.axis_size("tm")
    leading = lax.axis_index("tm") == 0
    leads = leading.astype(jnp.int32)[None]
    plane = primal.shape[3:]
    slab = struct(*primal.shape[1:])
    whole = struct(*primal.shape)
    share = struct(parts, FIELDS, 4, plane[1])
    room = pltpu.VMEM(slab.shape, jnp.float32)
    extra = pltpu.VMEM((2, FIELDS, HALO) + plane, jnp.float32)
    march_room = [room, room, extra, extra]
    packed = struct(FIELDS, PACKED, *plane)

    packed_room = pltpu.VMEM(packed.shape, jnp.float32)
    up, down = call(
        border_kernel,
        (packed, packed),
        (in_hbm(mixing), in_hbm(primal)),
        [SMEM, HBM],
        2 * PACKED,
        scratch=[packed_room, packed_room, pltpu.SemaphoreType.DMA((2 * STEPS,))],
    )
    packed_low, packed_high = exchange(up, down)
    first_source = source[0]
    primal, source = in_hbm(primal), in_hbm(source)
    stream = [pltpu.VMEM(whole.shape, jnp.float32), pltpu.SemaphoreType.DMA((STEPS,))]
    half, rest = struct(FIELDS, HALF, *plane), struct(FIELDS, STEPS - HALF, *plane)
    fewer = struct(FIELDS, STEPS - 1 - HALF, *plane)
    added = struct(2, FIELDS, HALO, *plane)

    def march_first(start, low, high, forced):
        later = (struct(STEPS - HALF - 1, *slab.shape),) if forced else ()
        return call(
            functools.partial(march_first_kernel, STEPS, forced),
            (slab, added) + later,
            (mixing, source, start, low, high, slope, packed_low, packed_high),
            [SMEM, HBM],
            42,
            scratch=march_room + stream,
        )

    slope_share, slope, up, down, up_rest, down_rest = call(
        guess_kernel,
        (share, whole, half, half, rest, rest),
        (mixing, primal, source, guess),
        [SMEM, HBM, HBM],
        100,
        scratch=[stream[0], stream[0], room, room, pltpu.VMEM(share.shape, jnp.float32), pltpu.SemaphoreType.DMA((2, STEPS))],
        first_out=HBM,
    )
    low, high = exchange(up, down)
    low_rest, high_rest = exchange(up_rest, down_rest)
    middle, middle_added, later = march_first(guess[0], low, high, True)
    (ended,) = call(
        end_kernel,
        (slab,),
        (mixing, later, middle, middle_added, low_rest, high_rest, slope, packed_low, packed_high),
        [SMEM],
        46,
        scratch=march_room,
    )
    ended = from_behind(ended)
    slope_shares = lax.all_to_all(slope_share, "tm", 0, 0)
    relaxed, change, middle, up, down = call(
        relaxed_kernel,
        (slab, slab, slab, half, half),
        (mixing, leads, source, ended, guess, slope),
        [SMEM, SMEM, HBM],
        30,
        scratch=[pltpu.VMEM((1,) + slab.shape, jnp.float32), room, room, room, stream[1]],
        first_out=HBM,
    )
    low, high = exchange(up, down)
    up_rest, down_rest = call(
        functools.partial(rest_kernel, STEPS, False),
        (rest, rest),
        (mixing, source, middle, slope),
        [SMEM, HBM],
        20,
        scratch=[room, room] + stream,
    )
    low_rest, high_rest = exchange(up_rest, down_rest)
    middle, middle_added = march_first(change, low, high, False)
    change, change_share = call(
        change_kernel,
        (slab, share),
        (mixing, leads, source, middle, middle_added, low_rest, high_rest, slope, packed_low, packed_high),
        [SMEM, SMEM, HBM],
        50,
        scratch=march_room + [pltpu.VMEM((1,) + slab.shape, jnp.float32), room, stream[1]],
        first_out=HBM,
    )
    change_shares = lax.all_to_all(change_share, "tm", 0, 0)
    residual = jnp.where(leading, first_source, from_behind(change))
    (error_shares,) = call(scan_kernel, (share,), (mixing, slope_shares, change_shares), [SMEM], 16)
    error_share = lax.all_to_all(error_shares, "tm", 0, 0)
    corrected, middle, up, down = call(
        corrected_kernel,
        (slab, slab, half, half),
        (mixing, leads, in_hbm(relaxed), source, error_share, slope),
        [SMEM, SMEM, HBM, HBM],
        30,
        scratch=[room, stream[0], room, room, pltpu.SemaphoreType.DMA((STEPS + 1,))],
    )
    low, high = exchange(up, down)
    up_rest, down_rest, upcoming = call(
        functools.partial(rest_kernel, STEPS - 1, True),
        (fewer, fewer, slab),
        (mixing, source, middle, slope),
        [SMEM, HBM],
        16,
        scratch=[room, room] + stream,
    )
    low_rest, high_rest = exchange(up_rest, down_rest)
    states_room = march_room + [stream[0], stream[0], stream[1], stream[1]]
    later = struct(STEPS - HALF - 1, *slab.shape)
    earlier, middle, middle_added, later = call(
        states_first_kernel,
        (whole, slab, added, later),
        (mixing, source, upcoming, corrected, low, high, slope, packed_low, packed_high),
        [SMEM, HBM],
        42,
        scratch=states_room,
        first_out=HBM,
    )
    (fine_states,) = call(
        states_rest_kernel,
        (whole,),
        (mixing, earlier, later, middle, middle_added, low_rest, high_rest, slope, packed_low, packed_high),
        [SMEM, HBM],
        34,
        scratch=march_room + [stream[0], stream[1]],
        first_out=HBM,
        alias={1: 0},
    )
    return fine_states, residual[None]


def solution(mesh):
    split = P("tm", None, "space", None, None)
    return jax.shard_map(
        per_device,
        mesh=mesh,
        in_specs=(split, split, split, P()),
        out_specs=(split, split),
        check_vma=False,
    )
```

```python
import functools

import jax
import jax.numpy as jnp
from jax import lax
from jax.experimental import pallas as pl
from jax.experimental.pallas import tpu as pltpu
from jax.sharding import PartitionSpec as P


STEPS = 8
FIELDS = 5
WIDE = 8
DIFFUSION = 0.1
RATE = 0.25
COARSE_STEP = 0.75
KEEP = 1.0 - 6.0 * DIFFUSION - RATE
REACH = [min(m, STEPS - 1 - m) for m in range(STEPS)]
REACH_AT = [sum(REACH[:m]) for m in range(STEPS)]
PACKED = sum(REACH)
HALF = STEPS // 2
HALO = max(min(m + 1, STEPS - 1 - m) for m in range(STEPS))


def mixed(mix, fields):
    out = []
    for i in range(FIELDS):
        total = mix[i][0] * fields[0]
        for j in range(1, FIELDS):
            total = total + mix[i][j] * fields[j]
        out.append(total)
    return out


def scalars(mix_ref):
    return [[mix_ref[i, j] for j in range(FIELDS)] for i in range(FIELDS)]


def wall_neighbours(v):
    row = lax.broadcasted_iota(jnp.int32, (8, 128), 0)
    first, last = row == 0, row == 7
    a, b = v[:8], v[8:]
    a_next, b_next = pltpu.roll(a, 1, 0), pltpu.roll(b, 1, 0)
    a_prev, b_prev = pltpu.roll(a, 7, 0), pltpu.roll(b, 7, 0)
    upper = jnp.where(first, 0.0, a_next) + jnp.where(last, b_prev, a_prev)
    lower = jnp.where(first, a_next, b_next) + jnp.where(last, 0.0, b_prev)
    return jnp.concatenate([upper, lower], axis=0)


def stepped(mix, field, beside, slope, source):
    out = []
    for f, turned in enumerate(mixed(mix, field)):
        v = field[f]
        around = pltpu.roll(v, 1, 1) + pltpu.roll(v, 127, 1) + wall_neighbours(v)
        around = around + beside[f]
        new = KEEP * v + DIFFUSION * around + slope[f] * turned
        out.append(new if source is None else new + source[f])
    return out


class Streamed:
    def __init__(self, hbm, room, sems, wanted):
        self.copies = {t: pltpu.make_async_copy(hbm.at[t], room.at[t], sems.at[t]) for t in wanted}
        for copy in self.copies.values():
            copy.start()

    def ready(self, t):
        if t in self.copies:
            self.copies.pop(t).wait()


def slopes(mix, state):
    out = []
    for value in mixed(mix, state):
        tilted = jnp.tanh(value)
        out.append(RATE - RATE * (tilted * tilted))
    return out


def border_kernel(mix_ref, primal_hbm, up_ref, down_ref, up_state, down_state, sems):
    mix = scalars(mix_ref)
    copies = []
    for m in range(STEPS):
        n, a = REACH[m], REACH_AT[m]
        if n > 0:
            ends = (pl.ds(WIDE - n, n), up_state), (pl.ds(0, n), down_state)
            for planes, state in ends:
                copies.append(
                    pltpu.make_async_copy(
                        primal_hbm.at[m, :, planes], state.at[:, a : a + n], sems.at[len(copies)]
                    )
                )
    for copy in copies:
        copy.start()
    for side, (state, out_ref) in enumerate(((up_state, up_ref), (down_state, down_ref))):
        for copy in copies[side::2]:
            copy.wait()

        def plane(n, carry):
            for k in range(4):
                x = 4 * n + k
                for f, value in enumerate(slopes(mix, [state[f, x] for f in range(FIELDS)])):
                    out_ref[f, x] = value
            return carry

        lax.fori_loop(0, PACKED // 4, plane, 0)


def shares(part):
    return [(part * x + q, x, 4 * q) for x in range(WIDE) for q in range(part)]


def alone_step(mix, m, here, there, slope_ref, source_ref, ends):
    for x in range(WIDE):
        if not (x >= m + 1 or x <= WIDE - 2 - m):
            continue
        field = [here[f, x] for f in range(FIELDS)]
        if x == 0:
            beside = [here[f, 1] for f in range(FIELDS)]
        elif x == WIDE - 1:
            beside = [here[f, WIDE - 2] for f in range(FIELDS)]
        else:
            beside = [here[f, x - 1] + here[f, x + 1] for f in range(FIELDS)]
        slope = [slope_ref[m, f, x] for f in range(FIELDS)]
        source = None
        if source_ref is not None:
            source = [source_ref[m + 1, f, x] for f in range(FIELDS)]
        new = stepped(mix, field, beside, slope, source)
        for f in range(FIELDS):
            there[f, x] = new[f]
            if x == 0 or x == WIDE - 1:
                ends[(m + 1) // HALF][int(x == 0)][f, (m + 1) % HALF] = new[f]


def guess_kernel(mix_ref, primal_hbm, source_hbm, guess_ref, share_hbm, slope_ref, up_one, down_one, up_two, down_two, primal, source_ref, one, two, share_ref, sems):
    mix = scalars(mix_ref)
    primal_in = Streamed(primal_hbm, primal, sems.at[0], range(STEPS))
    source_in = Streamed(source_hbm, source_ref, sems.at[1], range(1, STEPS))
    start_ref = guess_ref.at[0]
    ends = [(up_one, down_one), (up_two, down_two)]
    for f in range(FIELDS):
        down_one[f, 0] = start_ref[f, 0]
        up_one[f, 0] = start_ref[f, WIDE - 1]
    buffers = (one, two)
    for t in range(STEPS):
        primal_in.ready(t)

        def plane(n, carry):
            for k in range(2):
                x = 2 * n + k
                state = [primal[t, f, x] for f in range(FIELDS)]
                for f, value in enumerate(slopes(mix, state)):
                    slope_ref[t, f, x] = value
            return carry

        lax.fori_loop(0, WIDE // 2, plane, 0)
        if t == 0:
            for share, x, row in shares(4):
                for f in range(FIELDS):
                    share_ref[share, f] = slope_ref[0, f, x, row : row + 4]
            share_out = pltpu.make_async_copy(share_ref, share_hbm, sems.at[1, 0])
            share_out.start()
        source_in.ready(t + 1)
        if t + 1 < STEPS:
            here = start_ref if t == 0 else buffers[t % 2]
            alone_step(mix, t, here, buffers[(t + 1) % 2], slope_ref, source_ref, ends)
    share_out.wait()


def relaxed_kernel(mix_ref, leads_ref, source_hbm, ended_ref, guess_ref, slope_ref, relaxed_hbm, change_ref, middle_ref, up_ref, down_ref, source_ref, relaxed_ref, one, two, sems):
    source_in = Streamed(source_hbm, source_ref, sems, [0])
    mix = scalars(mix_ref)
    leads = leads_ref[0] == 1
    source_in.ready(0)
    for f in range(FIELDS):
        for x in range(WIDE):
            before = guess_ref[0, f, x]
            after = jnp.where(leads, before, ended_ref[f, x] + source_ref[0, f, x])
            relaxed_ref[f, x] = after
            change_ref[f, x] = after - before
        down_ref[f, 0] = change_ref[f, 0]
        up_ref[f, 0] = change_ref[f, WIDE - 1]
    relaxed_out = pltpu.make_async_copy(relaxed_ref, relaxed_hbm, sems.at[1])
    relaxed_out.start()
    buffers = (one, two)
    for m in range(HALF - 1):
        here = change_ref if m == 0 else buffers[m % 2]
        there = middle_ref if m == HALF - 2 else buffers[(m + 1) % 2]
        alone_step(mix, m, here, there, slope_ref, None, [(up_ref, down_ref)])
    relaxed_out.wait()


def rest_kernel(count, forced, mix_ref, source_hbm, middle_ref, slope_ref, up_ref, down_ref, *rest):
    next_ref, (one, two, source_ref, sems) = rest[0], rest[-4:]
    if forced:
        fetch = pltpu.make_async_copy(source_hbm.at[1], next_ref, sems.at[0])
        fetch.start()
    source_in = Streamed(source_hbm, source_ref, sems, range(HALF, count) if forced else [])
    mix = scalars(mix_ref)
    buffers = (one, two)
    for m in range(HALF - 1, count - 1):
        source_in.ready(m + 1)
        here = middle_ref if m == HALF - 1 else buffers[m % 2]
        source = source_ref if forced else None
        alone_step(mix, m, here, buffers[(m + 1) % 2], slope_ref, source, [None, (up_ref, down_ref)])
    if forced:
        fetch.wait()


def corrected_kernel(mix_ref, leads_ref, relaxed_hbm, source_hbm, share_ref, slope_ref, corrected_ref, middle_ref, up_ref, down_ref, relaxed_ref, source_ref, one, two, sems):
    relaxed_in = pltpu.make_async_copy(relaxed_hbm, relaxed_ref, sems.at[STEPS])
    relaxed_in.start()
    source_in = Streamed(source_hbm, source_ref, sems, range(HALF))
    mix = scalars(mix_ref)
    leads = leads_ref[0] == 1
    relaxed_in.wait()
    source_in.ready(0)
    for share, x, row in shares(4):
        for f in range(FIELDS):
            rows = slice(row, row + 4)
            error = jnp.where(leads, source_ref[0, f, x, rows], share_ref[share, f])
            corrected_ref[f, x, rows] = relaxed_ref[f, x, rows] + error
    for f in range(FIELDS):
        down_ref[f, 0] = corrected_ref[f, 0]
        up_ref[f, 0] = corrected_ref[f, WIDE - 1]
    buffers = (one, two)
    for m in range(HALF - 1):
        source_in.ready(m + 1)
        here = corrected_ref if m == 0 else buffers[m % 2]
        there = middle_ref if m == HALF - 2 else buffers[(m + 1) % 2]
        alone_step(mix, m, here, there, slope_ref, source_ref, [(up_ref, down_ref)])


def march_steps(count, steps, forced, done, step_opens, step_ends, mix, start_ref, start_added, low_ref, high_ref, slope_ref, source_ref, packed_low, packed_high, one, two, added_one, added_two, middle=None):
    fields = range(FIELDS)
    buffers, extras = (one, two), (added_one, added_two)
    sides = (
        (0, low_ref, packed_low, lambda n, p: n - p),
        (WIDE - 1, high_ref, packed_high, lambda n, p: p - 1),
    )
    for m in steps:
        here = start_ref if m == steps[0] else buffers[m % 2]
        step_opens(m)
        here_added = start_added if m == steps[0] else extras[m % 2]
        there, there_added = buffers[(m + 1) % 2], extras[(m + 1) % 2]
        if middle is not None and m == steps[-1]:
            there, there_added = middle
        last = m + 1 == count

        def own(x, beside):
            field = [here[f, x] for f in fields]
            slope = [slope_ref[m, f, x] for f in fields]
            source = [source_ref[m + 1, f, x] for f in fields] if forced and m + 1 < STEPS else None
            new = stepped(mix, field, beside, slope, source)
            for f in fields:
                if not last:
                    there[f, x] = new[f]
                done(m + 1, f, x, new[f])

        for side, (edge, alone, packed, place) in enumerate(sides):
            inner = edge + 1 if edge == 0 else edge - 1
            beyond = [alone[m // HALF][f, m % HALF] for f in fields]
            if m > 0:
                beyond = [beyond[f] + here_added[side, f, 0] for f in fields]
            own(edge, [here[f, inner] + beyond[f] for f in fields])
            for p in range(1, min(m + 1, count - 1 - m) + 1):
                nearer = [here[f, edge] if p == 1 else here_added[side, f, p - 2] for f in fields]
                if p == m + 1:
                    for f in fields:
                        there_added[side, f, p - 1] = DIFFUSION * nearer[f]
                    continue
                beside = nearer
                if p + 1 <= m:
                    beside = [nearer[f] + here_added[side, f, p] for f in fields]
                at = REACH_AT[m] + place(REACH[m], p)
                new = stepped(
                    mix,
                    [here_added[side, f, p - 1] for f in fields],
                    beside,
                    [packed[f, at] for f in fields],
                    None,
                )
                for f in fields:
                    there_added[side, f, p - 1] = new[f]

        def inside(i, carry):
            for k in range(3):
                x = 1 + 3 * i + k
                own(x, [here[f, x - 1] + here[f, x + 1] for f in fields])
            return carry

        lax.fori_loop(0, 2, inside, 0)
        step_ends(m)


def nothing(m):
    pass


def march_first_kernel(count, forced, mix_ref, source_hbm, start_ref, low_ref, high_ref, slope_ref, packed_low, packed_high, middle_ref, middle_added, *rest):
    later_ref, (one, two, added_one, added_two, source_ref, sems) = rest[0], rest[-6:]
    source_in = Streamed(source_hbm, source_ref, sems, range(1, HALF + 1) if forced else [])
    later = pltpu.make_async_copy(source_hbm.at[HALF + 1 :], later_ref, sems.at[HALF + 1]) if forced else None
    if forced:
        later.start()
    march_steps(
        count, range(HALF), forced, lambda *_: None, lambda m: source_in.ready(m + 1), nothing, scalars(mix_ref),
        start_ref, None, (low_ref, None), (high_ref, None), slope_ref, source_ref, packed_low, packed_high,
        one, two, added_one, added_two, (middle_ref, middle_added),
    )
    if forced:
        later.wait()


class Parts:
    def __init__(self, parts):
        self.parts = parts

    def __getitem__(self, index):
        return self.parts[index[0]][index[1:]]


def later_parts(ref):
    return {t: ref.at[t - HALF - 1] for t in range(HALF + 1, STEPS)}


def end_kernel(mix_ref, later_ref, middle_ref, middle_added, low_ref, high_ref, slope_ref, packed_low, packed_high, out_ref, one, two, added_one, added_two):
    def done(step, f, x, value):
        if step == STEPS:
            out_ref[f, x] = value

    march_steps(
        STEPS, range(HALF, STEPS), True, done, nothing, nothing, scalars(mix_ref),
        middle_ref, middle_added, (None, low_ref), (None, high_ref), slope_ref, Parts(later_parts(later_ref)), packed_low, packed_high,
        one, two, added_one, added_two,
    )


def change_kernel(mix_ref, leads_ref, source_hbm, middle_ref, middle_added, low_ref, high_ref, slope_ref, packed_low, packed_high, out_hbm, share_ref, one, two, added_one, added_two, source_ref, out_ref, sems):
    source_in = Streamed(source_hbm, source_ref, sems, [0])
    mix = scalars(mix_ref)

    def done(step, f, x, value):
        if step == STEPS:
            out_ref[f, x] = value

    march_steps(
        STEPS, range(HALF, STEPS), False, done, nothing, nothing, mix,
        middle_ref, middle_added, (None, low_ref), (None, high_ref), slope_ref, None, packed_low, packed_high,
        one, two, added_one, added_two,
    )
    out = pltpu.make_async_copy(out_ref, out_hbm, sems.at[1])
    out.start()
    for share, x, row in shares(4):
        for f in range(FIELDS):
            share_ref[share, f] = out_ref[f, x, row : row + 4]
    source_in.ready(0)

    @pl.when(leads_ref[0] == 1)
    def _():
        for x in range(WIDE):
            error = [source_ref[0, f, x] for f in range(FIELDS)]
            slope = [slope_ref[0, f, x] for f in range(FIELDS)]
            for f, moved in enumerate(coarse_turn(mix, error, slope)):
                value = moved + out_ref[f, x]
                for q in range(4):
                    share_ref[4 * x + q, f] = value[4 * q : 4 * q + 4]

    out.wait()


def states_first_kernel(mix_ref, source_hbm, next_ref, start_ref, low_ref, high_ref, slope_ref, packed_low, packed_high, out_hbm, middle_ref, middle_added, later_ref, one, two, added_one, added_two, source_ref, out_ref, sems, out_sems):
    source_in = Streamed(source_hbm, source_ref, sems, range(2, HALF + 1))
    parts = {1: next_ref} | {t: source_ref.at[t] for t in range(2, HALF + 1)}
    later = pltpu.make_async_copy(source_hbm.at[HALF + 1 :], later_ref, sems.at[HALF + 1])
    later.start()
    outs = [
        pltpu.make_async_copy(start_ref if t == 0 else out_ref.at[t], out_hbm.at[t], out_sems.at[t])
        for t in range(HALF)
    ]
    outs[0].start()

    def done(step, f, x, value):
        if step < HALF:
            out_ref[step, f, x] = value

    march_steps(
        STEPS - 1, range(HALF), True, done, lambda m: source_in.ready(m + 1), lambda m: outs[m + 1].start() if m + 1 < HALF else None,
        scalars(mix_ref),
        start_ref, None, (low_ref, None), (high_ref, None), slope_ref, Parts(parts), packed_low, packed_high,
        one, two, added_one, added_two, (middle_ref, middle_added),
    )
    later.wait()
    for out in outs:
        out.wait()


def states_rest_kernel(mix_ref, earlier_hbm, later_ref, middle_ref, middle_added, low_ref, high_ref, slope_ref, packed_low, packed_high, out_hbm, one, two, added_one, added_two, out_ref, out_sems):
    outs = {
        t: pltpu.make_async_copy(middle_ref if t == HALF else out_ref.at[t], out_hbm.at[t], out_sems.at[t])
        for t in range(HALF, STEPS)
    }
    outs[HALF].start()

    def done(step, f, x, value):
        out_ref[step, f, x] = value

    march_steps(
        STEPS - 1, range(HALF, STEPS - 1), True, done, nothing, lambda m: outs[m + 1].start(), scalars(mix_ref),
        middle_ref, middle_added, (None, low_ref), (None, high_ref), slope_ref, Parts(later_parts(later_ref)),
        packed_low, packed_high, one, two, added_one, added_two,
    )
    for out in outs.values():
        out.wait()


def coarse_turn(mix, error, slope):
    out = []
    for f, turned in enumerate(mixed(mix, error)):
        out.append((1.0 - COARSE_STEP) * error[f] + (COARSE_STEP / RATE) * slope[f] * turned)
    return out


def scan_kernel(mix_ref, slope_ref, resid_ref, error_ref):
    mix = scalars(mix_ref)
    blocks = resid_ref.shape[0]
    error = tuple(resid_ref[0, f] for f in range(FIELDS))
    for f in range(FIELDS):
        error_ref[0, f] = error[f]
        error_ref[1, f] = error[f]

    def turn(i, error):
        moved = coarse_turn(mix, error, [slope_ref[i, f] for f in range(FIELDS)])
        new = tuple(moved[f] + resid_ref[i, f] for f in range(FIELDS))
        for f in range(FIELDS):
            error_ref[i + 1, f] = new[f]
        return new

    lax.fori_loop(1, blocks - 1, turn, error, unroll=3 if (blocks - 2) % 3 == 0 else 1)


VMEM = pl.BlockSpec(memory_space=pltpu.VMEM)
SMEM = pl.BlockSpec(memory_space=pltpu.SMEM)
HBM = pl.BlockSpec(memory_space=pltpu.HBM)


def call(kernel, out, operands, places, planes, scratch=(), first_out=None, alias=None):
    read = sum(4 * operand.size for operand in operands)
    written = sum(4 * leaf.size for leaf in jax.tree.leaves(out))
    if first_out is not None:
        out = (pltpu.HBM(out[0].shape, out[0].dtype),) + tuple(out[1:])
    return pl.pallas_call(
        kernel,
        input_output_aliases=alias or {},
        out_shape=out,
        in_specs=places + [VMEM] * (len(operands) - len(places)),
        out_specs=[first_out or VMEM] + [VMEM] * (len(out) - 1),
        scratch_shapes=list(scratch),
        compiler_params=pltpu.CompilerParams(vmem_limit_bytes=20 << 20),
        cost_estimate=pl.CostEstimate(
            flops=planes * FIELDS * 2048 * 25, bytes_accessed=read + written, transcendentals=0
        ),
    )(*operands)


def in_hbm(array):
    return pltpu.with_memory_space_constraint(array, pltpu.HBM)


def struct(*shape):
    return jax.ShapeDtypeStruct(shape, jnp.float32)


def from_behind(array):
    count = lax.axis_size("tm")
    return lax.ppermute(array, "tm", [(i, i + 1) for i in range(count - 1)])


def exchange(up, down):
    count = lax.axis_size("space")
    forward = [(i, (i + 1) % count) for i in range(count)]
    backward = [(b, a) for a, b in forward]
    return lax.ppermute(up, "space", forward), lax.ppermute(down, "space", backward)


def per_device(primal, source, guess, mixing):
    parts = lax.axis_size("tm")
    leading = lax.axis_index("tm") == 0
    leads = leading.astype(jnp.int32)[None]
    plane = primal.shape[3:]
    slab = struct(*primal.shape[1:])
    whole = struct(*primal.shape)
    share = struct(parts, FIELDS, 4, plane[1])
    room = pltpu.VMEM(slab.shape, jnp.float32)
    extra = pltpu.VMEM((2, FIELDS, HALO) + plane, jnp.float32)
    march_room = [room, room, extra, extra]
    packed = struct(FIELDS, PACKED, *plane)

    packed_room = pltpu.VMEM(packed.shape, jnp.float32)
    up, down = call(
        border_kernel,
        (packed, packed),
        (in_hbm(mixing), in_hbm(primal)),
        [SMEM, HBM],
        2 * PACKED,
        scratch=[packed_room, packed_room, pltpu.SemaphoreType.DMA((2 * STEPS,))],
    )
    packed_low, packed_high = exchange(up, down)
    first_source = source[0]
    primal, source = in_hbm(primal), in_hbm(source)
    stream = [pltpu.VMEM(whole.shape, jnp.float32), pltpu.SemaphoreType.DMA((STEPS,))]
    half, rest = struct(FIELDS, HALF, *plane), struct(FIELDS, HALF - 1, *plane)
    added = struct(2, FIELDS, HALO, *plane)

    def march_first(start, low, high, forced):
        later = (struct(STEPS - HALF - 1, *slab.shape),) if forced else ()
        return call(
            functools.partial(march_first_kernel, STEPS, forced),
            (slab, added) + later,
            (mixing, source, start, low, high, slope, packed_low, packed_high),
            [SMEM, HBM],
            42,
            scratch=march_room + stream,
        )

    slope_share, slope, up, down, up_rest, down_rest = call(
        guess_kernel,
        (share, whole, half, half, half, half),
        (mixing, primal, source, guess),
        [SMEM, HBM, HBM],
        100,
        scratch=[stream[0], stream[0], room, room, pltpu.VMEM(share.shape, jnp.float32), pltpu.SemaphoreType.DMA((2, STEPS))],
        first_out=HBM,
    )
    low, high = exchange(up, down)
    low_rest, high_rest = exchange(up_rest, down_rest)
    middle, middle_added, later = march_first(guess[0], low, high, True)
    (ended,) = call(
        end_kernel,
        (slab,),
        (mixing, later, middle, middle_added, low_rest, high_rest, slope, packed_low, packed_high),
        [SMEM],
        46,
        scratch=march_room,
    )
    ended = from_behind(ended)
    slope_shares = lax.all_to_all(slope_share, "tm", 0, 0)
    relaxed, change, middle, up, down = call(
        relaxed_kernel,
        (slab, slab, slab, half, half),
        (mixing, leads, source, ended, guess, slope),
        [SMEM, SMEM, HBM],
        30,
        scratch=[pltpu.VMEM((1,) + slab.shape, jnp.float32), room, room, room, stream[1]],
        first_out=HBM,
    )
    low, high = exchange(up, down)
    up_rest, down_rest = call(
        functools.partial(rest_kernel, STEPS, False),
        (half, half),
        (mixing, source, middle, slope),
        [SMEM, HBM],
        20,
        scratch=[room, room] + stream,
    )
    low_rest, high_rest = exchange(up_rest, down_rest)
    middle, middle_added = march_first(change, low, high, False)
    change, change_share = call(
        change_kernel,
        (slab, share),
        (mixing, leads, source, middle, middle_added, low_rest, high_rest, slope, packed_low, packed_high),
        [SMEM, SMEM, HBM],
        50,
        scratch=march_room + [pltpu.VMEM((1,) + slab.shape, jnp.float32), room, stream[1]],
        first_out=HBM,
    )
    change_shares = lax.all_to_all(change_share, "tm", 0, 0)
    residual = jnp.where(leading, first_source, from_behind(change))
    (error_shares,) = call(scan_kernel, (share,), (mixing, slope_shares, change_shares), [SMEM], 16)
    error_share = lax.all_to_all(error_shares, "tm", 0, 0)
    corrected, middle, up, down = call(
        corrected_kernel,
        (slab, slab, half, half),
        (mixing, leads, in_hbm(relaxed), source, error_share, slope),
        [SMEM, SMEM, HBM, HBM],
        30,
        scratch=[room, stream[0], room, room, pltpu.SemaphoreType.DMA((STEPS + 1,))],
    )
    low, high = exchange(up, down)
    up_rest, down_rest, upcoming = call(
        functools.partial(rest_kernel, STEPS - 1, True),
        (rest, rest, slab),
        (mixing, source, middle, slope),
        [SMEM, HBM],
        16,
        scratch=[room, room] + stream,
    )
    low_rest, high_rest = exchange(up_rest, down_rest)
    states_room = march_room + [stream[0], stream[0], stream[1], stream[1]]
    later = struct(STEPS - HALF - 1, *slab.shape)
    earlier, middle, middle_added, later = call(
        states_first_kernel,
        (whole, slab, added, later),
        (mixing, source, upcoming, corrected, low, high, slope, packed_low, packed_high),
        [SMEM, HBM],
        42,
        scratch=states_room,
        first_out=HBM,
    )
    (fine_states,) = call(
        states_rest_kernel,
        (whole,),
        (mixing, earlier, later, middle, middle_added, low_rest, high_rest, slope, packed_low, packed_high),
        [SMEM, HBM],
        34,
        scratch=march_room + [stream[0], stream[1]],
        first_out=HBM,
        alias={1: 0},
    )
    return fine_states, residual[None]


def solution(mesh):
    split = P("tm", None, "space", None, None)
    return jax.shard_map(
        per_device,
        mesh=mesh,
        in_specs=(split, split, split, P()),
        out_specs=(split, split),
        check_vma=False,
    )
```
